256 devices in a mesh: rep: 16 (over z, core), row: 4 (over y), col: 4 (over x).
Axes of the slice: x: 4, y: 4, z: 8, core: 2. Of those that a mesh axis runs over, the one named last changes fastest.
Arguments:
- hidden_in: bfloat16 [16384, 2048], P(('rep', 'row', 'col')), may hold values from -6 to 6
- w_qkv: bfloat16 [2048, 16, 384], P(None, ('row', 'col')), may hold values from -0.125 to 0.125
- w_out: bfloat16 [16, 128, 2048], P(('row', 'col')), may hold values from -0.5 to 0.5
- w_gate_up: bfloat16 [2048, 2, 8192], P(None, None, ('row', 'col')), may hold values from -0.125 to 0.125
- w_down: bfloat16 [8192, 2048], P(('row', 'col')), may hold values from -0.0625 to 0.0625
- cache: bfloat16 [128, 2, 256, 16, 128], P('rep', None, None, ('row', 'col'))
- span_len: int32 [128], replicated, may hold values from 1 to 128, 8192 in all
- cache_len: int32 [128], replicated, may hold values from 1 to 256, 16384 in all
- new_slot: int32 [128], replicated, may hold values from 0 to 127, as said below
Outputs:
- hidden_out: bfloat16 [16384, 2048], P(('rep', 'row', 'col'))
- cache_out: bfloat16 [128, 2, 384, 16, 128], P('rep', None, None, ('row', 'col'))
The draws below stay inside these ranges and needn't reach their ends.
Inputs may be any that keep to these rules, and one draw needn't show every extreme that they name: A permutation of the 128 slots; slot s lies on replica s // 8, and new_slot[r] mod 8 equals r mod 8; the 8 requests of one replica go to at most 1 slots of any one replica, and some pair of replicas has exactly 1.
All inputs are finite; a program needn't handle non-finite values.
Results may differ from the reference program's by a relative error of at most 0.014.
The reference program's roundings to bfloat16 on the way (of `normed`, `values_new`, `weights`, `context`, `middle`, `normed_mid` and `hidden`) count: a program that leaves them out, or rounds other values in their place, can miss the bound.
Values may be sent and summed in bfloat16 or wider, within the bound.
No kernel may reach another device: no remote copies, remote signals or barrier semaphores. Data moves between devices by JAX's collectives and lax.ppermute only.
A program may use at most 128 MiB of HBM per device.

```python
import math
import jax
import jax.numpy as jnp
import numpy as np
from jax import lax

D = 2048
H = 16
HD = 128
FF = 8192
SLOTS = 8
SPAN = 128
CL = 256
REQS = 128


def draw_cache(key, part):
    normal_draw = jax.random.normal(key, (REQS, 2, CL, H, HD), jnp.float32)
    return normal_draw.astype(jnp.bfloat16)


def draw_new_slot(key, part):
    outer_key, inner_key, offset_key = jax.random.split(jax.random.fold_in(key, 7), 3)
    outer_perm = jax.random.permutation(outer_key, REQS // SLOTS)
    inner_perm = jax.random.permutation(inner_key, REQS // SLOTS)
    offset_perm = jax.random.permutation(offset_key, REQS // SLOTS)
    replica_ids = jnp.arange(REQS // SLOTS, dtype=jnp.int32)[:, None]
    slot_ids = jnp.arange(SLOTS, dtype=jnp.int32)[None, :]
    shifted = offset_perm[slot_ids % (REQS // SLOTS)]
    target_rep = outer_perm[(inner_perm[replica_ids] + shifted) % (REQS // SLOTS)]
    return (target_rep * SLOTS + slot_ids).reshape(REQS).astype(jnp.int32)


def level_of(key, shape, cuts, smallest, top_value):
    def one(axis_at, blocks):
        heights = jax.random.uniform(jax.random.fold_in(jax.random.fold_in(key, 6), axis_at), (blocks,), jnp.float32, smallest / len(cuts), top_value / len(cuts))
        return jnp.repeat(jnp.exp(heights), shape[axis_at] // blocks).reshape((-1,) + (1,) * (len(shape) - axis_at - 1))

    loudness = one(*cuts[0])
    for cut in cuts[1:]:
        loudness = loudness * one(*cut)
    return loudness


def profile(number_of, total, limit, lean):
    loads = [(1 << 20) // math.isqrt(grade ** lean) + 1 for grade in range(2, number_of + 1)]
    surplus, holding = total - limit - (number_of - 1), [1] * (number_of - 1)
    while surplus > 0:
        free = [i for i in range(number_of - 1) if holding[i] < limit]
        mass, remaining = sum([loads[i] for i in free]), surplus
        for i in free:
            more = min(limit - holding[i], max(1, remaining * loads[i] // mass), surplus)
            holding[i] = holding[i] + more
            surplus = surplus - more
    return np.array([limit] + holding)


def uneven(rng, count, total, limit, skew):
    if count == 2:
        one = jax.random.randint(rng, (), max(1, total - limit), min(limit, total - 1) + 1)
        return jnp.stack([one, total - one])
    lengths = jnp.asarray(profile(count, total, limit, skew), jnp.int32)
    pairs = (count - 1) // 2
    giver, taker = lengths[1:1 + 2 * pairs:2], lengths[2:2 + 2 * pairs:2]
    slack = jnp.minimum(giver - 1, limit - taker)
    moved = jax.random.randint(jax.random.fold_in(rng, 1), (pairs,), 0, 1 << 20) % (slack + 1)
    lengths = lengths.at[1:1 + 2 * pairs:2].set(giver - moved).at[2:2 + 2 * pairs:2].set(taker + moved)
    return lengths[jax.random.permutation(jax.random.fold_in(rng, 2), count)]


def bell_draw(key, extent, deviation, most, shards=(), kind=jnp.bfloat16):
    values = jax.random.normal(key, extent, jnp.float32) * deviation
    if len(shards) > 0:
        values = level_of(key, extent, shards, -0.22, 0.18) * values
    return jnp.clip(values, min=-most, max=most).astype(kind)


def setup_inputs(seed: int = 0) -> dict:
    seeds = jax.random.split(jax.random.key(seed), 10)
    return {
        "hidden_in": bell_draw(seeds[0], (REQS * SPAN, D), 1.0, 6.0, ((0, 256),)),
        "w_qkv": bell_draw(seeds[1], (D, H, 3 * HD), D ** -0.5, 0.125, ((1, 16),)),
        "w_out": bell_draw(seeds[2], (H, HD, D), HD ** -0.5, 0.5, ((0, 16),)),
        "w_gate_up": bell_draw(seeds[3], (D, 2, FF), D ** -0.5, 0.125, ((2, 16),)),
        "w_down": bell_draw(seeds[4], (FF, D), FF ** -0.5, 0.0625, ((0, 16),)),
        "cache": draw_cache(jax.random.fold_in(seeds[9], 71), 0),
        "span_len": uneven(seeds[6], REQS, REQS * SPAN // 2, SPAN, 2).astype(jnp.int32),
        "cache_len": uneven(seeds[7], REQS, REQS * CL // 2, CL, 1).astype(jnp.int32),
        "new_slot": draw_new_slot(jax.random.fold_in(seeds[9], 71), 0),
    }


EPSILON = 1e-05

def layer_norm(values):
    centred = values - lax.optimization_barrier(jnp.mean(values, axis=-1, keepdims=True))
    spread = lax.optimization_barrier(jnp.mean(centred * centred, axis=-1, keepdims=True))
    return centred * lax.rsqrt(spread + EPSILON)

def rotate(values, positions):
    halfway = values.shape[-1] // 2
    frequency = 10000.0 ** (-(jnp.arange(halfway, dtype=jnp.float32) * 2.0 / values.shape[-1]))
    angles = positions[..., None] * frequency
    cosine = jnp.cos(angles)
    sine_part = jnp.sin(angles)
    first_half = values[..., :halfway]
    second_half = values[..., halfway:]
    return jnp.concatenate([first_half * cosine - second_half * sine_part, second_half * cosine + first_half * sine_part], axis=-1)

def attend_one(operands):
    queries, keys_new, values_new, cache_old, length_old = operands
    total_keys = jnp.concatenate([cache_old[0], keys_new], axis=0).astype(jnp.float32)
    total_values = jnp.concatenate([cache_old[1], values_new], axis=0).astype(jnp.float32)
    scores = jnp.einsum('thd,shd->hts', queries.astype(jnp.float32), total_keys) * (1.0 / math.sqrt(queries.shape[-1]))
    source_pos = jnp.arange(total_keys.shape[0], dtype=jnp.int32)
    query_pos = jnp.arange(queries.shape[0], dtype=jnp.int32)
    stored = cache_old.shape[1]
    allowed = jnp.where(source_pos[None, :] < stored, source_pos[None, :] < length_old, source_pos[None, :] - stored <= query_pos[:, None])
    masked_scores = jnp.where(allowed[None], scores, -1e+30)
    highest = lax.optimization_barrier(jnp.max(masked_scores, axis=-1, keepdims=True))
    exponent = jnp.where(allowed[None], jnp.exp(masked_scores - highest), 0.0)
    weights = (exponent / lax.optimization_barrier(jnp.sum(exponent, axis=-1, keepdims=True))).astype(jnp.bfloat16)
    return jnp.einsum('hts,shd->thd', weights.astype(jnp.float32), total_values).astype(jnp.bfloat16)

def assemble_one(operands):
    old_rows, new_rows, length_old = operands
    zero_index = jnp.zeros((), jnp.int32)
    extended = jnp.concatenate([old_rows, jnp.zeros_like(new_rows)], axis=1)
    placed = lax.dynamic_update_slice(jnp.zeros_like(extended), new_rows, (zero_index, length_old.astype(jnp.int32), zero_index, zero_index))
    return extended + placed

def reference(hidden_in, w_qkv, w_out, w_gate_up, w_down, cache, span_len, cache_len, new_slot):
    inputs = hidden_in.astype(jnp.float32)
    normed = layer_norm(inputs).astype(jnp.bfloat16)
    joined = jnp.dot(normed, w_qkv.reshape(D, H * 3 * HD), preferred_element_type=jnp.float32).reshape(REQS, SPAN, H, 3, HD)
    offsets = jnp.arange(SPAN, dtype=jnp.int32)
    positions = (cache_len[:, None] + offsets[None, :]).astype(jnp.float32)[:, :, None]
    queries = rotate(joined[:, :, :, 0], positions).astype(jnp.bfloat16)
    keys_new = rotate(joined[:, :, :, 1], positions).astype(jnp.bfloat16)
    values_new = joined[:, :, :, 2].astype(jnp.bfloat16)
    context = lax.map(attend_one, (queries, keys_new, values_new, cache, cache_len))
    attention = jnp.dot(context.reshape(REQS * SPAN, H * HD), w_out.reshape(H * HD, D), preferred_element_type=jnp.float32)
    middle = (inputs + attention).astype(jnp.bfloat16)
    normed_mid = layer_norm(middle.astype(jnp.float32)).astype(jnp.bfloat16)
    gate_up = jnp.dot(normed_mid, w_gate_up.reshape(D, 2 * FF), preferred_element_type=jnp.float32)
    hidden = (jax.nn.silu(gate_up[:, :FF]) * gate_up[:, FF:]).astype(jnp.bfloat16)
    down_sum = jnp.dot(hidden, w_down, preferred_element_type=jnp.float32)
    live_rows = (offsets[None, :] < span_len[:, None]).reshape(REQS * SPAN, 1)
    hidden_out = jnp.where(live_rows, middle.astype(jnp.float32) + down_sum, 0.0).astype(jnp.bfloat16)
    stored_rows = jnp.arange(CL, dtype=jnp.int32)
    old_kept = jnp.where((stored_rows[None, :] < cache_len[:, None])[:, None, :, None, None], cache, 0.0)
    new_kv = jnp.stack([keys_new, values_new], axis=1)
    new_kept = jnp.where((offsets[None, :] < span_len[:, None])[:, None, :, None, None], new_kv, 0.0)
    appended = lax.map(assemble_one, (old_kept, new_kept, cache_len))
    cache_out = jnp.zeros_like(appended).at[new_slot].set(appended)
    return (hidden_out, cache_out)
```

```python
import math

import jax
import jax.numpy as jnp
from jax import lax
from jax.experimental import pallas as pl
from jax.experimental.pallas import tpu as pltpu
from jax.sharding import PartitionSpec as P

EPSILON = 1e-05
SHIFTS = (1, 3, 2)


def layer_norm(values):
    centred = values - jnp.mean(values, axis=-1, keepdims=True)
    spread = jnp.mean(centred * centred, axis=-1, keepdims=True)
    return centred * lax.rsqrt(spread + EPSILON)


def hop(axis, shift, array):
    size = lax.axis_size(axis)
    pairs = [(i, (i + shift) % size) for i in range(size)]
    return lax.ppermute(array, axis, pairs)


def gather_pair(first, second, first_axis, second_axis):
    got = {}
    for shift in SHIFTS:
        got[0, shift] = hop(first_axis, shift, first)
        got[1, shift] = hop(second_axis, shift, second)
    keys = list(got)
    held = lax.optimization_barrier([got[key] for key in keys])
    got = dict(zip(keys, held))
    return tuple(
        jnp.stack([own, got[n, 1], got[n, 2], got[n, 3]], axis=0)
        for n, own in enumerate((first, second))
    )


def gather_halves(rows):
    half, width = rows.shape[0] // 2, rows.shape[1]
    one, two = gather_pair(rows[:half], rows[half:], "col", "row")
    one, two = gather_pair(
        one.reshape(4 * half, width), two.reshape(4 * half, width), "row", "col"
    )
    return one.reshape(16 * half, width), two.reshape(16 * half, width)


def scatter_pair(first, second, first_axis, second_axis):
    got = {}
    for shift in SHIFTS:
        got[0, shift] = hop(first_axis, -shift, first[shift])
        got[1, shift] = hop(second_axis, -shift, second[shift])
    keys = list(got)
    held = lax.optimization_barrier([got[key] for key in keys])
    got = dict(zip(keys, held))
    sums = []
    for n, own in enumerate((first[0], second[0])):
        total = own.astype(jnp.float32)
        for shift in (1, 2, 3):
            total = total + got[n, shift].astype(jnp.float32)
        sums.append(total)
    return sums


def scatter_halves(one, two):
    half, width = one.shape[0] // 16, one.shape[1]
    one, two = scatter_pair(
        one.reshape(4, 4 * half, width), two.reshape(4, 4 * half, width), "row", "col"
    )
    one, two = scatter_pair(
        one.astype(jnp.bfloat16).reshape(4, half, width),
        two.astype(jnp.bfloat16).reshape(4, half, width),
        "col",
        "row",
    )
    return jnp.concatenate([one, two], axis=0)


def place_kernel(target_ref, cache_ref, out_ref):
    out_ref[...] = cache_ref[...]


def place_old(cache, targets, replicas):
    slots, kinds, stored, size = cache.shape
    return pl.pallas_call(
        place_kernel,
        out_shape=jax.ShapeDtypeStruct((replicas, kinds, stored, size), cache.dtype),
        grid_spec=pltpu.PrefetchScalarGridSpec(
            num_scalar_prefetch=1,
            grid=(slots,),
            in_specs=[pl.BlockSpec((1, kinds, stored, size), lambda s, t: (s, 0, 0, 0))],
            out_specs=pl.BlockSpec((1, kinds, stored, size), lambda s, t: (t[s], 0, 0, 0)),
        ),
        cost_estimate=pl.CostEstimate(
            flops=0, transcendentals=0, bytes_accessed=2 * cache.size * 2
        ),
        name="place_old",
    )(targets, cache)


def attend_kernel(
    meta_ref, one_ref, two_ref, cache_ref, cos_ref, sin_ref, context_ref, new_ref
):
    g = pl.program_id(0)

    def entry(n):
        return meta_ref[16 * g + n]

    length_old = entry(2)

    def block(ref, n):
        return ref[pl.ds(pl.multiple_of(32 * entry(n), 32), 32), :]

    joined = jnp.concatenate(
        [block(one_ref, 3), block(two_ref, 5), block(one_ref, 4), block(two_ref, 6)], axis=0
    )
    cosine, sine = cos_ref[0], sin_ref[0]

    def turned(part):
        return (part * cosine + pltpu.roll(part, 64, axis=1) * sine).astype(jnp.bfloat16)

    queries = turned(joined[:, :128])
    keys_new = turned(joined[:, 128:256])
    values_new = joined[:, 256:].astype(jnp.bfloat16)
    new_ref[0, 0] = keys_new
    new_ref[0, 1] = values_new
    scale = 1.0 / math.sqrt(128)
    contract = (((1,), (1,)), ((), ()))
    old = (
        lax.dot_general(queries, cache_ref[0, 0], contract, preferred_element_type=jnp.float32)
        * scale
    )
    new = (
        lax.dot_general(queries, keys_new, contract, preferred_element_type=jnp.float32) * scale
    )
    old_ok = lax.broadcasted_iota(jnp.int32, old.shape, 1) < length_old
    new_ok = lax.broadcasted_iota(jnp.int32, new.shape, 1) <= lax.broadcasted_iota(
        jnp.int32, new.shape, 0
    )
    old = jnp.where(old_ok, old, -1e30)
    new = jnp.where(new_ok, new, -1e30)
    highest = jnp.maximum(
        jnp.max(old, axis=1, keepdims=True), jnp.max(new, axis=1, keepdims=True)
    )
    old = jnp.where(old_ok, jnp.exp(old - highest), 0.0)
    new = jnp.where(new_ok, jnp.exp(new - highest), 0.0)
    total = jnp.sum(old, axis=1, keepdims=True) + jnp.sum(new, axis=1, keepdims=True)
    old_weights = (old / total).astype(jnp.bfloat16)
    new_weights = (new / total).astype(jnp.bfloat16)
    stored_values = cache_ref[0, 1]
    context = jnp.dot(
        old_weights, stored_values, preferred_element_type=jnp.float32
    ) + jnp.dot(new_weights, values_new, preferred_element_type=jnp.float32)
    context = context.astype(jnp.bfloat16)
    for n in range(2):
        place = pl.multiple_of(64 * entry(7 + n), 64)
        context_ref[pl.ds(place, 64), :] = context[64 * n : 64 * n + 64]


def attend(meta, one, two, cache, cosine, sine, replicas):
    slots, kinds, stored, size = cache.shape
    span = cosine.shape[1]
    whole = lambda g, m: (0, 0)
    mine = lambda g, m: (m[16 * g], 0, 0)
    return pl.pallas_call(
        attend_kernel,
        out_shape=(
            jax.ShapeDtypeStruct((slots * span, size), jnp.bfloat16),
            jax.ShapeDtypeStruct((replicas, kinds, span, size), jnp.bfloat16),
        ),
        grid_spec=pltpu.PrefetchScalarGridSpec(
            num_scalar_prefetch=1,
            grid=(slots,),
            in_specs=[
                pl.BlockSpec(one.shape, whole),
                pl.BlockSpec(two.shape, whole),
                pl.BlockSpec((1, kinds, stored, size), lambda g, m: (m[16 * g], 0, 0, 0)),
                pl.BlockSpec((1, span, size), mine),
                pl.BlockSpec((1, span, size), mine),
            ],
            out_specs=[
                pl.BlockSpec((slots * span, size), whole),
                pl.BlockSpec((1, kinds, span, size), lambda g, m: (m[16 * g + 1], 0, 0, 0)),
            ],
        ),
        cost_estimate=pl.CostEstimate(
            flops=4 * slots * span * (stored + span) * size,
            transcendentals=slots * span * (stored + span),
            bytes_accessed=6 << 20,
        ),
        name="attend",
    )(meta, one, two, cache, cosine, sine)


def append_kernel(source_ref, length_ref, span_ref, old_ref, new_ref, out_ref):
    t = pl.program_id(0)
    length, span = length_ref[t], span_ref[t]
    stored, fresh = old_ref.shape[2], new_ref.shape[2]
    size = old_ref.shape[3]
    live = lax.broadcasted_iota(jnp.int32, (fresh, size), 0) < span
    rows = lax.broadcasted_iota(jnp.int32, (stored + fresh, size), 0)
    for kind in range(2):
        new = jnp.where(live, new_ref[0, kind].astype(jnp.float32), 0.0)
        new = jnp.concatenate([new, jnp.zeros((stored, size), jnp.float32)], axis=0)
        old = jnp.concatenate(
            [old_ref[0, kind].astype(jnp.float32), jnp.zeros((fresh, size), jnp.float32)], axis=0
        )
        moved = pltpu.roll(new, length, axis=0)
        out_ref[0, kind] = jnp.where(rows < length, old, moved).astype(jnp.bfloat16)


def append(old, new, source, lengths, spans):
    slots = source.shape[0]
    _, kinds, stored, size = old.shape
    fresh = new.shape[2]
    take = lambda t, s, l, n: (s[t], 0, 0, 0)
    return pl.pallas_call(
        append_kernel,
        out_shape=jax.ShapeDtypeStruct((slots, kinds, stored + fresh, size), jnp.bfloat16),
        grid_spec=pltpu.PrefetchScalarGridSpec(
            num_scalar_prefetch=3,
            grid=(slots,),
            in_specs=[
                pl.BlockSpec((1, kinds, stored, size), take),
                pl.BlockSpec((1, kinds, fresh, size), take),
            ],
            out_specs=pl.BlockSpec(
                (1, kinds, stored + fresh, size), lambda t, s, l, n: (t, 0, 0, 0)
            ),
        ),
        cost_estimate=pl.CostEstimate(
            flops=0, transcendentals=0, bytes_accessed=4 * slots * kinds * (stored + fresh) * size
        ),
        name="append",
    )(source, lengths, spans, old, new)


def attend_table(targets, lengths, row, column):
    step = jnp.arange(8, dtype=jnp.int32)
    request = 2 * ((row + step // 2) % 4) + step % 2
    source_row = request // 2
    back = (row - source_row) % 4
    fields = [request, targets[request], lengths[request]]
    columns = [2 * (request % 2), 2 * (request % 2) + 1]
    fields += [4 * back + (column - c) % 4 for c in columns]
    fields += [4 * ((column - c) % 4) + back for c in columns]
    fields += [4 * (step // 2) + (c - column) % 4 for c in columns]
    fields += [jnp.zeros_like(step)] * (16 - len(fields))
    return jnp.stack(fields, axis=1).reshape(-1)


def body(hidden_in, w_qkv, w_out, w_gate_up, w_down, cache, span_len, cache_len, new_slot):
    slots, kinds, stored, _, size = cache.shape
    local_rows, width = hidden_in.shape
    units = w_down.shape[0]
    span = 16 * local_rows // slots
    replica = lax.axis_index("rep")
    replicas = lax.axis_size("rep")
    row, column = lax.axis_index("row"), lax.axis_index("col")
    cache = cache.reshape(slots, kinds, stored, size)
    lengths = lax.dynamic_slice_in_dim(cache_len, replica * slots, slots)
    spans = lax.dynamic_slice_in_dim(span_len, replica * slots, slots)
    targets = lax.dynamic_slice_in_dim(new_slot, replica * slots, slots) // slots
    my_slots = replica * slots + jnp.arange(slots, dtype=jnp.int32)
    arrivals = (new_slot[None, :] == my_slots[:, None]).astype(jnp.int32)
    requests = jnp.arange(new_slot.shape[0], dtype=jnp.int32)
    source = jnp.sum(arrivals * (requests // slots)[None, :], axis=1)
    arrived_length = jnp.sum(arrivals * cache_len[None, :], axis=1)
    arrived_span = jnp.sum(arrivals * span_len[None, :], axis=1)

    heads_out = lax.all_gather(w_out.reshape(size, width), "row", axis=0, tiled=False)
    old_sent = place_old(cache, targets, replicas)
    old_moved = lax.all_to_all(old_sent, "rep", split_axis=0, concat_axis=0, tiled=True)

    inputs = hidden_in.astype(jnp.float32)
    normed = layer_norm(inputs).astype(jnp.bfloat16)
    one, two = gather_halves(normed)
    heads = w_qkv.reshape(width, 3 * size)
    joined_one = jnp.dot(one, heads, preferred_element_type=jnp.float32)
    joined_two = jnp.dot(two, heads, preferred_element_type=jnp.float32)

    offsets = jnp.arange(span, dtype=jnp.int32)
    positions = (lengths[:, None] + offsets[None, :]).astype(jnp.float32)
    frequency = 10000.0 ** (-(jnp.arange(size // 2, dtype=jnp.float32) * 2.0 / size))
    angles = positions[:, :, None] * frequency
    cosine, sine = jnp.cos(angles), jnp.sin(angles)
    cosine = jnp.concatenate([cosine, cosine], axis=-1)
    sine = jnp.concatenate([-sine, sine], axis=-1)
    meta = attend_table(targets, lengths, row, column)
    context, new_sent = attend(meta, joined_one, joined_two, cache, cosine, sine, replicas)
    new_moved = lax.all_to_all(new_sent, "rep", split_axis=0, concat_axis=0, tiled=True)

    context = context.reshape(4, 4 * local_rows, size)
    parts = [context[0]] + [hop("row", k, context[k]) for k in (1, 2, 3)]
    back = (row - jnp.arange(4, dtype=jnp.int32)) % 4
    w_rows = jnp.take(heads_out, back, axis=0).reshape(4 * size, width)
    partial = jnp.dot(
        jnp.concatenate(parts, axis=1), w_rows, preferred_element_type=jnp.float32
    ).astype(jnp.bfloat16)
    partial = partial.reshape(4, local_rows, width)
    attention = partial[0].astype(jnp.float32)
    for k in (1, 2, 3):
        attention = attention + hop("col", k, partial[k]).astype(jnp.float32)
    middle = (inputs + attention).astype(jnp.bfloat16)
    normed_mid = layer_norm(middle.astype(jnp.float32)).astype(jnp.bfloat16)

    one, two = gather_halves(normed_mid)
    w_in = w_gate_up.reshape(width, 2 * units)

    def feed_forward(rows):
        gate_up = jnp.dot(rows, w_in, preferred_element_type=jnp.float32)
        hidden = (jax.nn.silu(gate_up[:, :units]) * gate_up[:, units:]).astype(jnp.bfloat16)
        return jnp.dot(hidden, w_down, preferred_element_type=jnp.float32).astype(jnp.bfloat16)

    down_sum = scatter_halves(feed_forward(one), feed_forward(two))

    cache_out = append(old_moved, new_moved, source, arrived_length, arrived_span)
    first_row = (row * 4 + column) * local_rows
    within = first_row % span + jnp.arange(local_rows, dtype=jnp.int32)
    live = within < lax.dynamic_index_in_dim(spans, first_row // span, keepdims=False)
    hidden_out = jnp.where(live[:, None], middle.astype(jnp.float32) + down_sum, 0.0)
    return (
        hidden_out.astype(jnp.bfloat16),
        cache_out.reshape(slots, kinds, stored + span, 1, size),
    )


def solution(mesh):
    in_specs = (
        P(("rep", "row", "col"), None),
        P(None, ("row", "col"), None),
        P(("row", "col"), None, None),
        P(None, None, ("row", "col")),
        P(("row", "col"), None),
        P("rep", None, None, ("row", "col"), None),
        P(),
        P(),
        P(),
    )
    out_specs = (P(("rep", "row", "col"), None), P("rep", None, None, ("row", "col"), None))
    return jax.shard_map(body, mesh=mesh, in_specs=in_specs, out_specs=out_specs, check_vma=False)
```

```python
import math

import jax
import jax.numpy as jnp
from jax import lax
from jax.experimental import pallas as pl
from jax.experimental.pallas import tpu as pltpu
from jax.sharding import PartitionSpec as P

EPSILON = 1e-05


def layer_norm(values):
    centred = values - jnp.mean(values, axis=-1, keepdims=True)
    spread = jnp.mean(centred * centred, axis=-1, keepdims=True)
    return centred * lax.rsqrt(spread + EPSILON)


def swap(axis, k, array):
    size = lax.axis_size(axis)
    return lax.ppermute(array, axis, [(i, i ^ k) for i in range(size)])


def together(sent):
    got = [swap(axis, k, array) for axis, k, array in sent]
    return lax.optimization_barrier(got)


def gather_plane(rows, extra):
    half = rows.shape[0] // 2
    one, two = rows[:half], rows[half:]
    with_extra = jnp.concatenate([two, extra], axis=0)
    got = together([x for k in (1, 3, 2) for x in (("col", k, one), ("row", k, with_extra))])
    extra = jnp.stack([extra, got[1][half:], got[5][half:], got[3][half:]], axis=0)
    one = jnp.concatenate([one, got[0], got[4], got[2]], axis=0)
    two = jnp.concatenate([two, got[1][:half], got[5][:half], got[3][:half]], axis=0)
    got = together([x for k in (1, 3, 2) for x in (("row", k, one), ("col", k, two))])
    one = jnp.concatenate([one, got[0], got[4], got[2]], axis=0)
    two = jnp.concatenate([two, got[1], got[5], got[3]], axis=0)
    return one, two, extra


def gather_block(rows):
    half = rows.shape[0] // 2
    one, two = rows[:half], rows[half:]
    got = together([("col", 1, one), ("row", 1, two), ("col", 3, one), ("col", 2, one)])
    one = jnp.concatenate([one, got[0], got[3], got[2]], axis=0)
    two = jnp.concatenate([two, got[1]], axis=0)
    got = together([("row", 1, one), ("col", 1, two), ("col", 3, two), ("col", 2, two)])
    return jnp.concatenate([one, got[0], two, got[1], got[3], got[2]], axis=0)


def wide_sum(arrays):
    total = arrays[0].astype(jnp.float32)
    for array in arrays[1:]:
        total = total + array.astype(jnp.float32)
    return total


def scatter_block(sums, half):
    one = [sums[4 * half * n : 4 * half * (n + 1)] for n in range(2)]
    two = [sums[8 * half + 2 * half * n : 8 * half + 2 * half * (n + 1)] for n in range(4)]
    got = together([("row", 1, one[1]), ("col", 1, two[1]), ("col", 3, two[3]), ("col", 2, two[2])])
    one = wide_sum([one[0], got[0]]).astype(jnp.bfloat16)
    two = wide_sum([two[0], got[1], got[3], got[2]]).astype(jnp.bfloat16)
    one = [one[half * n : half * (n + 1)] for n in range(4)]
    two = [two[half * n : half * (n + 1)] for n in range(2)]
    got = together([("col", 1, one[1]), ("row", 1, two[1]), ("col", 3, one[3]), ("col", 2, one[2])])
    return jnp.concatenate(
        [wide_sum([one[0], got[0], got[3], got[2]]), wide_sum([two[0], got[1]])], axis=0
    )


def attend_kernel(
    meta_ref, one_ref, two_ref, cache_ref, cos_ref, sin_ref, context_ref, new_ref
):
    g = pl.program_id(0)

    def entry(n):
        return meta_ref[16 * g + n]

    length_old = entry(2)

    def block(ref, n):
        return ref[pl.ds(pl.multiple_of(32 * entry(n), 32), 32), :]

    joined = jnp.concatenate(
        [block(one_ref, 3), block(two_ref, 5), block(one_ref, 4), block(two_ref, 6)], axis=0
    )
    cosine, sine = cos_ref[0], sin_ref[0]

    def turned(part):
        return (part * cosine + pltpu.roll(part, 64, axis=1) * sine).astype(jnp.bfloat16)

    queries = turned(joined[:, :128])
    keys_new = turned(joined[:, 128:256])
    values_new = joined[:, 256:].astype(jnp.bfloat16)
    stored = cache_ref.shape[2]
    whole = new_ref.shape[2]
    live = lax.broadcasted_iota(jnp.int32, keys_new.shape, 0) < entry(9)
    rows = lax.broadcasted_iota(jnp.int32, (whole, keys_new.shape[1]), 0)
    for kind, fresh in enumerate((keys_new, values_new)):
        fresh = jnp.where(live, fresh.astype(jnp.float32), 0.0)
        fresh = jnp.concatenate(
            [fresh, jnp.zeros((whole - fresh.shape[0], fresh.shape[1]), jnp.float32)], axis=0
        )
        old = cache_ref[0, kind].astype(jnp.float32)
        old = jnp.concatenate(
            [old, jnp.zeros((whole - stored, old.shape[1]), jnp.float32)], axis=0
        )
        fresh = pltpu.roll(fresh, length_old, axis=0)
        new_ref[0, kind] = jnp.where(rows < length_old, old, fresh).astype(jnp.bfloat16)
    scale = 1.0 / math.sqrt(128)
    contract = (((1,), (1,)), ((), ()))
    old = (
        lax.dot_general(queries, cache_ref[0, 0], contract, preferred_element_type=jnp.float32)
        * scale
    )
    new = (
        lax.dot_general(queries, keys_new, contract, preferred_element_type=jnp.float32) * scale
    )
    old_ok = lax.broadcasted_iota(jnp.int32, old.shape, 1) < length_old
    new_ok = lax.broadcasted_iota(jnp.int32, new.shape, 1) <= lax.broadcasted_iota(
        jnp.int32, new.shape, 0
    )
    old = jnp.where(old_ok, old, -1e30)
    new = jnp.where(new_ok, new, -1e30)
    highest = jnp.maximum(
        jnp.max(old, axis=1, keepdims=True), jnp.max(new, axis=1, keepdims=True)
    )
    old = jnp.where(old_ok, jnp.exp(old - highest), 0.0)
    new = jnp.where(new_ok, jnp.exp(new - highest), 0.0)
    total = jnp.sum(old, axis=1, keepdims=True) + jnp.sum(new, axis=1, keepdims=True)
    old_weights = (old / total).astype(jnp.bfloat16)
    new_weights = (new / total).astype(jnp.bfloat16)
    stored_values = cache_ref[0, 1]
    context = jnp.dot(
        old_weights, stored_values, preferred_element_type=jnp.float32
    ) + jnp.dot(new_weights, values_new, preferred_element_type=jnp.float32)
    context = context.astype(jnp.bfloat16)
    for n in range(2):
        place = pl.multiple_of(64 * entry(7 + n), 64)
        context_ref[pl.ds(place, 64), :] = context[64 * n : 64 * n + 64]


def attend(meta, one, two, cache, cosine, sine, replicas):
    slots, kinds, stored, size = cache.shape
    span = cosine.shape[1]
    whole = lambda g, m: (0, 0)
    mine = lambda g, m: (m[16 * g], 0, 0)
    return pl.pallas_call(
        attend_kernel,
        out_shape=(
            jax.ShapeDtypeStruct((slots * span, size), jnp.bfloat16),
            jax.ShapeDtypeStruct((replicas, kinds, stored + span, size), jnp.bfloat16),
        ),
        grid_spec=pltpu.PrefetchScalarGridSpec(
            num_scalar_prefetch=1,
            grid=(slots,),
            in_specs=[
                pl.BlockSpec(one.shape, whole),
                pl.BlockSpec(two.shape, whole),
                pl.BlockSpec((1, kinds, stored, size), lambda g, m: (m[16 * g], 0, 0, 0)),
                pl.BlockSpec((1, span, size), mine),
                pl.BlockSpec((1, span, size), mine),
            ],
            out_specs=[
                pl.BlockSpec((slots * span, size), whole),
                pl.BlockSpec(
                    (1, kinds, stored + span, size), lambda g, m: (m[16 * g + 1], 0, 0, 0)
                ),
            ],
        ),
        cost_estimate=pl.CostEstimate(
            flops=4 * slots * span * (stored + span) * size,
            transcendentals=slots * span * (stored + span),
            bytes_accessed=6 << 20,
        ),
        name="attend",
    )(meta, one, two, cache, cosine, sine)


def pick_kernel(source_ref, moved_ref, out_ref, sems):
    copies = [
        pltpu.make_async_copy(moved_ref.at[source_ref[t]], out_ref.at[t], sems.at[t])
        for t in range(out_ref.shape[0])
    ]
    for copy in copies:
        copy.start()
    for copy in copies:
        copy.wait()


def pick(moved, source):
    shape = (source.shape[0],) + moved.shape[1:]
    return pl.pallas_call(
        pick_kernel,
        out_shape=jax.ShapeDtypeStruct(shape, moved.dtype),
        in_specs=[pl.BlockSpec(memory_space=pltpu.SMEM), pl.BlockSpec(memory_space=pl.ANY)],
        out_specs=pl.BlockSpec(memory_space=pl.ANY),
        scratch_shapes=[pltpu.SemaphoreType.DMA((shape[0],))],
        cost_estimate=pl.CostEstimate(
            flops=0, transcendentals=0, bytes_accessed=4 * math.prod(shape)
        ),
        name="pick",
    )(source, moved)


def attend_table(targets, lengths, spans, row, column):
    step = jnp.arange(8, dtype=jnp.int32)
    request = 2 * (row ^ (step // 2)) + step % 2
    away = row ^ (request // 2)
    fields = [request, targets[request], lengths[request]]
    columns = [column ^ (2 * (request % 2)), column ^ (2 * (request % 2) + 1)]
    fields += [4 * away + c for c in columns]
    fields += [4 * c + away for c in columns]
    fields += [4 * (step // 2) + c for c in columns]
    fields += [spans[request]]
    fields += [jnp.zeros_like(step)] * (16 - len(fields))
    return jnp.stack(fields, axis=1).reshape(-1)


def body(hidden_in, w_qkv, w_out, w_gate_up, w_down, cache, span_len, cache_len, new_slot):
    slots, kinds, stored, _, size = cache.shape
    local_rows, width = hidden_in.shape
    units = w_down.shape[0]
    span = 16 * local_rows // slots
    replica = lax.axis_index("rep")
    replicas = lax.axis_size("rep")
    row, column = lax.axis_index("row"), lax.axis_index("col")
    cache = cache.reshape(slots, kinds, stored, size)
    lengths = lax.dynamic_slice_in_dim(cache_len, replica * slots, slots)
    spans = lax.dynamic_slice_in_dim(span_len, replica * slots, slots)
    targets = lax.dynamic_slice_in_dim(new_slot, replica * slots, slots) // slots
    my_slots = replica * slots + jnp.arange(slots, dtype=jnp.int32)
    arrivals = (new_slot[None, :] == my_slots[:, None]).astype(jnp.int32)
    requests = jnp.arange(new_slot.shape[0], dtype=jnp.int32)
    source = jnp.sum(arrivals * (requests // slots)[None, :], axis=1)

    share = size // replicas
    out_slice = lax.dynamic_slice_in_dim(w_out.reshape(size, width), replica * share, share)
    rows_in, rows_down = width // replicas, units // replicas
    in_slice = lax.dynamic_slice_in_dim(w_gate_up, replica * rows_in, rows_in)
    down_slice = lax.dynamic_slice_in_dim(w_down, replica * rows_down, rows_down)
    feed_slice = jnp.concatenate(
        [in_slice.reshape(rows_in, 2 * units), down_slice[:, : 2 * units], down_slice[:, 2 * units :]],
        axis=0,
    )

    inputs = hidden_in.astype(jnp.float32)
    normed = layer_norm(inputs).astype(jnp.bfloat16)
    one, two, out_slices = gather_plane(normed, out_slice)
    w_rows = lax.all_gather(out_slices, "rep", axis=1, tiled=True).reshape(4 * size, width)
    w_in = w_gate_up.reshape(width, 2 * units)
    one, two, w_in, feed_slice = lax.optimization_barrier((one, two, w_in, feed_slice))
    feed_far = swap("row", 2, feed_slice)
    heads = w_qkv.reshape(width, 3 * size)
    joined_one = jnp.dot(one, heads, preferred_element_type=jnp.float32)
    joined_two = jnp.dot(two, heads, preferred_element_type=jnp.float32)

    offsets = jnp.arange(span, dtype=jnp.int32)
    positions = (lengths[:, None] + offsets[None, :]).astype(jnp.float32)
    frequency = 10000.0 ** (-(jnp.arange(size // 2, dtype=jnp.float32) * 2.0 / size))
    angles = positions[:, :, None] * frequency
    cosine, sine = jnp.cos(angles), jnp.sin(angles)
    cosine = jnp.concatenate([cosine, cosine], axis=-1)
    sine = jnp.concatenate([-sine, sine], axis=-1)
    meta = attend_table(targets, lengths, spans, row, column)
    context, sent = attend(meta, joined_one, joined_two, cache, cosine, sine, replicas)
    context, feed_far = lax.optimization_barrier((context, feed_far))
    fed = lax.all_gather(feed_far, "rep", axis=0, tiled=False)
    w_in_far = fed[:, :rows_in].reshape(width, 2 * units)
    w_down_far = jnp.concatenate(
        [fed[:, rows_in : rows_in + rows_down], fed[:, rows_in + rows_down :]], axis=2
    ).reshape(units, width)

    context = context.reshape(4, 4 * local_rows, size)
    got = together([("row", k, context[k]) for k in (1, 3, 2)])
    parts = jnp.concatenate([context[0], got[0], got[2], got[1]], axis=1)
    partial = jnp.dot(parts, w_rows, preferred_element_type=jnp.float32).astype(jnp.bfloat16)
    partial = partial.reshape(4, local_rows, width)
    got = together([("col", k, partial[k]) for k in (1, 3, 2)])
    middle = (inputs + wide_sum([partial[0], got[0], got[2], got[1]])).astype(jnp.bfloat16)
    normed_mid = layer_norm(middle.astype(jnp.float32)).astype(jnp.bfloat16)

    moved = lax.all_to_all(sent, "rep", split_axis=0, concat_axis=0, tiled=True)

    tokens = gather_block(normed_mid)
    down_sum = jnp.zeros((tokens.shape[0], width), jnp.float32)
    for w_in, w_back in ((w_in, w_down), (w_in_far, w_down_far)):
        gate_up = jnp.dot(tokens, w_in, preferred_element_type=jnp.float32)
        hidden = (jax.nn.silu(gate_up[:, :units]) * gate_up[:, units:]).astype(jnp.bfloat16)
        down_sum = down_sum + jnp.dot(hidden, w_back, preferred_element_type=jnp.float32)
    down_sum = scatter_block(down_sum.astype(jnp.bfloat16), local_rows // 2)

    cache_out = pick(moved, source)
    first_row = (row * 4 + column) * local_rows
    within = first_row % span + jnp.arange(local_rows, dtype=jnp.int32)
    live = within < lax.dynamic_index_in_dim(spans, first_row // span, keepdims=False)
    hidden_out = jnp.where(live[:, None], middle.astype(jnp.float32) + down_sum, 0.0)
    return (
        hidden_out.astype(jnp.bfloat16),
        cache_out.reshape(slots, kinds, stored + span, 1, size),
    )


def solution(mesh):
    in_specs = (
        P(("rep", "row", "col"), None),
        P(None, ("row", "col"), None),
        P(("row", "col"), None, None),
        P(None, None, ("row", "col")),
        P(("row", "col"), None),
        P("rep", None, None, ("row", "col"), None),
        P(),
        P(),
        P(),
    )
    out_specs = (P(("rep", "row", "col"), None), P("rep", None, None, ("row", "col"), None))
    return jax.shard_map(body, mesh=mesh, in_specs=in_specs, out_specs=out_specs, check_vma=False)
```

```python
import math

import jax
import jax.numpy as jnp
import numpy as np
from jax import lax
from jax.experimental import pallas as pl
from jax.experimental.pallas import tpu as pltpu
from jax.sharding import PartitionSpec as P

EPSILON = 1e-05


def layer_norm(values):
    centred = values - jnp.mean(values, axis=-1, keepdims=True)
    spread = jnp.mean(centred * centred, axis=-1, keepdims=True)
    return centred * lax.rsqrt(spread + EPSILON)


def swap(axis, k, array):
    size = lax.axis_size(axis)
    return lax.ppermute(array, axis, [(i, i ^ k) for i in range(size)])


def together(sent):
    got = [swap(axis, k, array) for axis, k, array in sent]
    return lax.optimization_barrier(got)


def join(pieces):
    return lax.optimization_barrier(jnp.concatenate(pieces, axis=0))


def gather_plane(one, two, half):
    got = together([x for k in (1, 3, 2) for x in (("col", k, one), ("row", k, two))])
    extra = jnp.stack([two[half:], got[1][half:], got[5][half:], got[3][half:]], axis=0)
    one = join([one, got[0], got[4], got[2]])
    two = join([two[:half], got[1][:half], got[5][:half], got[3][:half]])
    got = together([x for k in (1, 3, 2) for x in (("row", k, one), ("col", k, two))])
    return [one, got[0], got[4], got[2], two, got[1], got[5], got[3]], extra


def gather_block(one, two):
    got = together([("col", 1, one), ("row", 1, two), ("col", 3, one), ("col", 2, one)])
    two = join([two, got[1]])
    one = join([one, got[0], got[3], got[2]])
    got = together([("col", 1, two), ("row", 1, one), ("col", 3, two), ("col", 2, two)])
    return [one, got[1], two, got[0], got[3], got[2]]


def wide_sum(arrays):
    total = arrays[0].astype(jnp.float32)
    for array in arrays[1:]:
        total = total + array.astype(jnp.float32)
    return total


def scatter_block(sums, half):
    one, two = sums[:2], sums[2:]
    got = together([("col", 1, two[1]), ("row", 1, one[1]), ("col", 3, two[3]), ("col", 2, two[2])])
    one = wide_sum([one[0], got[1]]).astype(jnp.bfloat16)
    two = wide_sum([two[0], got[0], got[3], got[2]]).astype(jnp.bfloat16)
    one = [one[half * n : half * (n + 1)] for n in range(4)]
    two = [two[half * n : half * (n + 1)] for n in range(2)]
    got = together([("col", 1, one[1]), ("row", 1, two[1]), ("col", 3, one[3]), ("col", 2, one[2])])
    return jnp.concatenate(
        [wide_sum([one[0], got[0], got[3], got[2]]), wide_sum([two[0], got[1]])], axis=0
    )


def norm_kernel(rows_ref, extra_ref, one_ref, two_ref):
    half = one_ref.shape[0]
    normed = layer_norm(rows_ref[...].astype(jnp.float32)).astype(jnp.bfloat16)
    one_ref[...] = normed[:half]
    two_ref[:half] = normed[half:]
    two_ref[half:] = extra_ref[...]


def norm(rows, extra):
    half, width = rows.shape[0] // 2, rows.shape[1]
    return pl.pallas_call(
        norm_kernel,
        out_shape=(
            jax.ShapeDtypeStruct((half, width), jnp.bfloat16),
            jax.ShapeDtypeStruct((half + extra.shape[0], width), jnp.bfloat16),
        ),
        cost_estimate=pl.CostEstimate(
            flops=8 * rows.size, transcendentals=0, bytes_accessed=4 * rows.size
        ),
        name="norm",
    )(rows, extra)


def mid_kernel(rows_ref, own_ref, a_ref, b_ref, c_ref, middle_ref, one_ref, two_ref):
    half = one_ref.shape[0]
    attention = wide_sum([own_ref[...], a_ref[...], b_ref[...], c_ref[...]])
    middle = (rows_ref[...].astype(jnp.float32) + attention).astype(jnp.bfloat16)
    middle_ref[...] = middle
    normed = layer_norm(middle.astype(jnp.float32)).astype(jnp.bfloat16)
    one_ref[...] = normed[:half]
    two_ref[...] = normed[half:]


def mid(rows, own, others):
    half, width = rows.shape[0] // 2, rows.shape[1]
    part = jax.ShapeDtypeStruct((half, width), jnp.bfloat16)
    return pl.pallas_call(
        mid_kernel,
        out_shape=(jax.ShapeDtypeStruct(rows.shape, jnp.bfloat16), part, part),
        cost_estimate=pl.CostEstimate(
            flops=12 * rows.size, transcendentals=0, bytes_accessed=14 * rows.size
        ),
        name="mid",
    )(rows, own, *others)


def joined_kernel(*refs):
    pieces, (heads_ref, out_ref, rows_ref, sems) = refs[:8], refs[8:]
    tall = pieces[0].shape[0]
    copies = [
        pltpu.make_async_copy(piece, rows_ref.at[pl.ds(tall * n, tall)], sems.at[n])
        for n, piece in enumerate(pieces)
    ]
    for copy in copies:
        copy.start()
    for n in range(4):
        copies[2 * n].wait()
        copies[2 * n + 1].wait()
        span = pl.ds(2 * tall * n, 2 * tall)
        out_ref[span, :] = jnp.dot(
            rows_ref[span, :], heads_ref[...], preferred_element_type=jnp.float32
        )


def join_heads(pieces, heads):
    tall, width = pieces[0].shape
    shape = (len(pieces) * tall, heads.shape[1])
    return pl.pallas_call(
        joined_kernel,
        out_shape=jax.ShapeDtypeStruct(shape, jnp.float32),
        in_specs=[pl.BlockSpec(memory_space=pl.ANY)] * len(pieces)
        + [pl.BlockSpec(memory_space=pltpu.VMEM)],
        out_specs=pl.BlockSpec(memory_space=pltpu.VMEM),
        scratch_shapes=[
            pltpu.VMEM((shape[0], width), jnp.bfloat16),
            pltpu.SemaphoreType.DMA((len(pieces),)),
        ],
        compiler_params=pltpu.CompilerParams(vmem_limit_bytes=24 << 20),
        cost_estimate=pl.CostEstimate(
            flops=2 * shape[0] * width * shape[1], transcendentals=0, bytes_accessed=7 << 20
        ),
        name="join_heads",
    )(*pieces, heads)


def feed_kernel(*refs):
    pieces, (w_in_ref, w_down_ref, fed_ref), outs = refs[:6], refs[6:9], refs[9:15]
    rows_ref, in_ref, down_ref, hidden_ref, sems = refs[15:]
    units, width = w_down_ref.shape
    shares, tall, _ = fed_ref.shape
    part_in, part_down = width // shares, units // shares
    jobs, at = [], 0
    for piece in pieces:
        jobs.append((piece, rows_ref.at[pl.ds(at, piece.shape[0])]))
        at += piece.shape[0]
    jobs.append((w_in_ref, in_ref.at[0]))
    jobs.append((w_down_ref, down_ref.at[0]))
    half = width // 2
    for r in range(shares):
        jobs.append(
            (fed_ref.at[r, pl.ds(0, part_in)], in_ref.at[1, pl.ds(part_in * r, part_in)])
        )
        for n in range(2):
            jobs.append(
                (
                    fed_ref.at[r, pl.ds(part_in + part_down * n, part_down)],
                    down_ref.at[1, pl.ds(part_down * r, part_down), pl.ds(half * n, half)],
                )
            )
    copies = [
        pltpu.make_async_copy(source, target, sems.at[n])
        for n, (source, target) in enumerate(jobs)
    ]
    for copy in copies:
        copy.start()
    for n, copy in enumerate(copies):
        if n < 7:
            copy.wait()
    step = 256
    for shard in range(2):
        if shard == 1:
            for copy in copies[7:]:
                copy.wait()

        @pl.loop(0, units // step)
        def _(j):
            at = pl.multiple_of(step * j, step)
            gate = jnp.dot(
                rows_ref[...],
                in_ref[shard, :, pl.ds(at, step)],
                preferred_element_type=jnp.float32,
            )
            up = jnp.dot(
                rows_ref[...],
                in_ref[shard, :, pl.ds(pl.multiple_of(units + at, step), step)],
                preferred_element_type=jnp.float32,
            )
            hidden = gate / (1.0 + jnp.exp(-gate)) * up
            hidden_ref[shard, :, pl.ds(at, step)] = hidden.astype(jnp.bfloat16)

    @pl.loop(0, width // step)
    def _(j):
        span = pl.ds(pl.multiple_of(step * j, step), step)
        total = jnp.dot(
            hidden_ref[0], down_ref[0, :, span], preferred_element_type=jnp.float32
        ) + jnp.dot(hidden_ref[1], down_ref[1, :, span], preferred_element_type=jnp.float32)
        total = total.astype(jnp.bfloat16)
        at = 0
        for out in outs:
            out[:, span] = total[at : at + out.shape[0]]
            at += out.shape[0]


def feed(pieces, w_in, w_down, fed):
    units, width = w_down.shape
    rows = sum(piece.shape[0] for piece in pieces)
    return pl.pallas_call(
        feed_kernel,
        out_shape=[jax.ShapeDtypeStruct(piece.shape, jnp.bfloat16) for piece in pieces],
        in_specs=[pl.BlockSpec(memory_space=pl.ANY)] * (len(pieces) + 3),
        out_specs=[pl.BlockSpec(memory_space=pltpu.VMEM)] * len(pieces),
        scratch_shapes=[
            pltpu.VMEM((rows, width), jnp.bfloat16),
            pltpu.VMEM((2, width, 2 * units), jnp.bfloat16),
            pltpu.VMEM((2, units, width), jnp.bfloat16),
            pltpu.VMEM((2, rows, units), jnp.bfloat16),
            pltpu.SemaphoreType.DMA((len(pieces) + 2 + 3 * fed.shape[0],)),
        ],
        compiler_params=pltpu.CompilerParams(vmem_limit_bytes=48 << 20),
        cost_estimate=pl.CostEstimate(
            flops=12 * rows * width * units, transcendentals=2 * rows * units,
            bytes_accessed=16 << 20,
        ),
        name="feed",
    )(*pieces, w_in, w_down, fed)


def attend_kernel(
    place_ref, length_ref, span_ref, target_ref,
    joined_ref, cache_ref, cos_ref, sin_ref, far_cos_ref, far_sin_ref, context_ref, new_ref,
):
    g = pl.program_id(0)
    row, column = place_ref[0], place_ref[1]
    request = request_of(g, row)
    length_old = length_ref[request]
    away = row ^ (request // 2)
    columns = [column ^ (2 * (request % 2) + n) for n in range(2)]

    def block(n):
        return joined_ref[pl.ds(pl.multiple_of(32 * n, 32), 32), :]

    joined = jnp.concatenate(
        [block(n) for c in columns for n in (4 * away + c, 16 + 4 * c + away)], axis=0
    )
    far_cos, far_sin = far_cos_ref[pl.ds(request, 1), :], far_sin_ref[pl.ds(request, 1), :]
    cosine = far_cos * cos_ref[...] - far_sin * sin_ref[...]
    sine = far_sin * cos_ref[...] + far_cos * sin_ref[...]

    def turned(part):
        return (part * cosine + pltpu.roll(part, 64, axis=1) * sine).astype(jnp.bfloat16)

    queries = turned(joined[:, :128])
    keys_new = turned(joined[:, 128:256])
    values_new = joined[:, 256:].astype(jnp.bfloat16)
    stored = cache_ref.shape[2]
    whole = new_ref.shape[2]
    live = lax.broadcasted_iota(jnp.int32, keys_new.shape, 0) < span_ref[request]
    rows = lax.broadcasted_iota(jnp.int32, (whole, keys_new.shape[1]), 0)
    for kind, fresh in enumerate((keys_new, values_new)):
        fresh = jnp.where(live, fresh.astype(jnp.float32), 0.0)
        fresh = jnp.concatenate(
            [fresh, jnp.zeros((whole - fresh.shape[0], fresh.shape[1]), jnp.float32)], axis=0
        )
        old = cache_ref[0, kind].astype(jnp.float32)
        old = jnp.concatenate(
            [old, jnp.zeros((whole - stored, old.shape[1]), jnp.float32)], axis=0
        )
        fresh = pltpu.roll(fresh, length_old, axis=0)
        new_ref[0, kind] = jnp.where(rows < length_old, old, fresh).astype(jnp.bfloat16)
    scale = 1.0 / math.sqrt(128)
    contract = (((1,), (1,)), ((), ()))
    old = (
        lax.dot_general(queries, cache_ref[0, 0], contract, preferred_element_type=jnp.float32)
        * scale
    )
    new = (
        lax.dot_general(queries, keys_new, contract, preferred_element_type=jnp.float32) * scale
    )
    old_ok = lax.broadcasted_iota(jnp.int32, old.shape, 1) < length_old
    new_ok = lax.broadcasted_iota(jnp.int32, new.shape, 1) <= lax.broadcasted_iota(
        jnp.int32, new.shape, 0
    )
    old = jnp.where(old_ok, old, -1e30)
    new = jnp.where(new_ok, new, -1e30)
    highest = jnp.maximum(
        jnp.max(old, axis=1, keepdims=True), jnp.max(new, axis=1, keepdims=True)
    )
    old = jnp.where(old_ok, jnp.exp(old - highest), 0.0)
    new = jnp.where(new_ok, jnp.exp(new - highest), 0.0)
    total = jnp.sum(old, axis=1, keepdims=True) + jnp.sum(new, axis=1, keepdims=True)
    old_weights = (old / total).astype(jnp.bfloat16)
    new_weights = (new / total).astype(jnp.bfloat16)
    stored_values = cache_ref[0, 1]
    context = jnp.dot(
        old_weights, stored_values, preferred_element_type=jnp.float32
    ) + jnp.dot(new_weights, values_new, preferred_element_type=jnp.float32)
    context = context.astype(jnp.bfloat16)
    for n in range(2):
        place = pl.multiple_of(64 * (4 * (g // 2) + columns[n]), 64)
        context_ref[pl.ds(place, 64), :] = context[64 * n : 64 * n + 64]


def request_of(g, row):
    return 2 * (row ^ (g // 2)) + g % 2


def attend(place, lengths, spans, targets, joined, cache, tables, replicas):
    slots, kinds, stored, size = cache.shape
    span = tables[0].shape[0]
    whole = lambda g, *refs: (0, 0)
    return pl.pallas_call(
        attend_kernel,
        out_shape=(
            jax.ShapeDtypeStruct((slots * span, size), jnp.bfloat16),
            jax.ShapeDtypeStruct((replicas, kinds, stored + span, size), jnp.bfloat16),
        ),
        grid_spec=pltpu.PrefetchScalarGridSpec(
            num_scalar_prefetch=4,
            grid=(slots,),
            in_specs=[
                pl.BlockSpec(joined.shape, whole),
                pl.BlockSpec(
                    (1, kinds, stored, size),
                    lambda g, place, *refs: (request_of(g, place[0]), 0, 0, 0),
                ),
            ]
            + [pl.BlockSpec(table.shape, whole) for table in tables],
            out_specs=[
                pl.BlockSpec((slots * span, size), whole),
                pl.BlockSpec(
                    (1, kinds, stored + span, size),
                    lambda g, place, lengths, spans, targets: (
                        targets[request_of(g, place[0])], 0, 0, 0,
                    ),
                ),
            ],
        ),
        cost_estimate=pl.CostEstimate(
            flops=4 * slots * span * (stored + span) * size,
            transcendentals=slots * span * (stored + span),
            bytes_accessed=6 << 20,
        ),
        name="attend",
    )(place, lengths, spans, targets, joined, cache, *tables)


def pick_kernel(source_ref, moved_ref, out_ref, held_ref, sems):
    slots = out_ref.shape[0]
    taken = [
        pltpu.make_async_copy(moved_ref.at[source_ref[t]], held_ref.at[t], sems.at[0, t])
        for t in range(slots)
    ]
    given = [
        pltpu.make_async_copy(held_ref.at[t], out_ref.at[t], sems.at[1, t]) for t in range(slots)
    ]
    for copy in taken:
        copy.start()
    for t in range(slots):
        taken[t].wait()
        given[t].start()
    for copy in given:
        copy.wait()


def pick(moved, source):
    shape = (source.shape[0],) + moved.shape[1:]
    return pl.pallas_call(
        pick_kernel,
        out_shape=jax.ShapeDtypeStruct(shape, moved.dtype),
        in_specs=[pl.BlockSpec(memory_space=pltpu.SMEM), pl.BlockSpec(memory_space=pl.ANY)],
        out_specs=pl.BlockSpec(memory_space=pl.ANY),
        scratch_shapes=[pltpu.VMEM(shape, moved.dtype), pltpu.SemaphoreType.DMA((2, shape[0]))],
        cost_estimate=pl.CostEstimate(
            flops=0, transcendentals=0, bytes_accessed=4 * math.prod(shape)
        ),
        name="pick",
    )(source, moved)


def body(hidden_in, w_qkv, w_out, w_gate_up, w_down, cache, span_len, cache_len, new_slot):
    slots, kinds, stored, _, size = cache.shape
    local_rows, width = hidden_in.shape
    units = w_down.shape[0]
    span = 16 * local_rows // slots
    replica = lax.axis_index("rep")
    replicas = lax.axis_size("rep")
    row, column = lax.axis_index("row"), lax.axis_index("col")
    cache = cache.reshape(slots, kinds, stored, size)
    lengths = lax.dynamic_slice_in_dim(cache_len, replica * slots, slots)
    spans = lax.dynamic_slice_in_dim(span_len, replica * slots, slots)
    targets = lax.dynamic_slice_in_dim(new_slot, replica * slots, slots) // slots
    my_slots = replica * slots + jnp.arange(slots, dtype=jnp.int32)
    arrivals = (new_slot[None, :] == my_slots[:, None]).astype(jnp.int32)
    requests = jnp.arange(new_slot.shape[0], dtype=jnp.int32)
    source = jnp.sum(arrivals * (requests // slots)[None, :], axis=1)

    share = size // replicas
    out_slice = lax.dynamic_slice_in_dim(w_out.reshape(size, width), replica * share, share)
    rows_in, rows_down = width // replicas, units // replicas
    in_slice = lax.dynamic_slice_in_dim(w_gate_up, replica * rows_in, rows_in)
    down_slice = lax.dynamic_slice_in_dim(w_down, replica * rows_down, rows_down)
    feed_slice = jnp.concatenate(
        [in_slice.reshape(rows_in, 2 * units), down_slice[:, : 2 * units], down_slice[:, 2 * units :]],
        axis=0,
    )

    one, two = norm(hidden_in, out_slice)
    pieces, out_slices = gather_plane(one, two, local_rows // 2)
    w_rows = lax.all_gather(out_slices, "rep", axis=1, tiled=True).reshape(4 * size, width)
    w_in = w_gate_up.reshape(width, 2 * units)
    pieces, w_in, feed_slice = lax.optimization_barrier((pieces, w_in, feed_slice))
    feed_far = swap("row", 2, feed_slice)
    joined = join_heads(pieces, w_qkv.reshape(width, 3 * size))
    joined, feed_far = lax.optimization_barrier((joined, feed_far))
    fed = lax.all_gather(feed_far, "rep", axis=0, tiled=False)

    frequency = 10000.0 ** (-(np.arange(size // 2) * 2.0 / size))
    frequency = np.concatenate([frequency, frequency])[None, :]
    sign = np.where(np.arange(size) < size // 2, -1.0, 1.0)[None, :]
    near = np.arange(span)[:, None] * frequency
    far = lengths.astype(jnp.float32)[:, None] * jnp.asarray(frequency, jnp.float32)
    tables = (
        jnp.asarray(np.cos(near), jnp.float32),
        jnp.asarray(np.sin(near) * sign, jnp.float32),
        jnp.cos(far),
        jnp.sin(far) * jnp.asarray(sign, jnp.float32),
    )
    place = jnp.stack([row, column]).astype(jnp.int32)
    context, sent = attend(place, lengths, spans, targets, joined, cache, tables, replicas)

    context = context.reshape(4, 4 * local_rows, size)
    got = together([("row", k, context[k]) for k in (1, 3, 2)])
    parts = jnp.concatenate([context[0], got[0], got[2], got[1]], axis=1)
    partial = jnp.dot(parts, w_rows, preferred_element_type=jnp.float32).astype(jnp.bfloat16)
    partial = partial.reshape(4, local_rows, width)
    got = together([("col", k, partial[k]) for k in (1, 3, 2)])
    middle, one, two = mid(hidden_in, partial[0], [got[0], got[2], got[1]])
    moved = lax.all_to_all(sent, "rep", split_axis=0, concat_axis=0, tiled=True)
    sums = feed(gather_block(one, two), w_in, w_down, fed)
    down_sum = scatter_block(sums, local_rows // 2)

    cache_out = pick(moved, source)
    first_row = (row * 4 + column) * local_rows
    within = first_row % span + jnp.arange(local_rows, dtype=jnp.int32)
    live = within < lax.dynamic_index_in_dim(spans, first_row // span, keepdims=False)
    hidden_out = jnp.where(live[:, None], middle.astype(jnp.float32) + down_sum, 0.0)
    return (
        hidden_out.astype(jnp.bfloat16),
        cache_out.reshape(slots, kinds, stored + span, 1, size),
    )


def solution(mesh):
    in_specs = (
        P(("rep", "row", "col"), None),
        P(None, ("row", "col"), None),
        P(("row", "col"), None, None),
        P(None, None, ("row", "col")),
        P(("row", "col"), None),
        P("rep", None, None, ("row", "col"), None),
        P(),
        P(),
        P(),
    )
    out_specs = (P(("rep", "row", "col"), None), P("rep", None, None, ("row", "col"), None))
    return jax.shard_map(body, mesh=mesh, in_specs=in_specs, out_specs=out_specs, check_vma=False)
```

```python
import math

import jax
import jax.numpy as jnp
import numpy as np
from jax import lax
from jax.experimental import pallas as pl
from jax.experimental.pallas import tpu as pltpu
from jax.sharding import PartitionSpec as P

EPSILON = 1e-05


def layer_norm(values):
    centred = values - jnp.mean(values, axis=-1, keepdims=True)
    spread = jnp.mean(centred * centred, axis=-1, keepdims=True)
    return centred * lax.rsqrt(spread + EPSILON)


def swap(axis, k, array):
    size = lax.axis_size(axis)
    return lax.ppermute(array, axis, [(i, i ^ k) for i in range(size)])


def together(sent):
    got = [swap(axis, k, array) for axis, k, array in sent]
    return lax.optimization_barrier(got)


def join(pieces):
    return lax.optimization_barrier(jnp.concatenate(pieces, axis=0))


def gather_plane(one, two, also):
    sent = [x for k in (1, 3, 2) for x in (("col", k, one), ("row", k, two))]
    got = lax.optimization_barrier([swap(*x) for x in sent] + also)
    also = got[6:]
    one = join([one, got[0], got[4], got[2]])
    two = join([two, got[1], got[5], got[3]])
    got = together([x for k in (1, 3, 2) for x in (("row", k, one), ("col", k, two))])
    return [one, got[0], got[4], got[2], two, got[1], got[5], got[3]], also


def gather_block(one, two):
    got = together([("col", 1, one), ("row", 1, two), ("col", 3, one), ("col", 2, one)])
    two = join([two, got[1]])
    one = join([one, got[0], got[3], got[2]])
    got = together([("col", 1, two), ("row", 1, one), ("col", 3, two), ("col", 2, two)])
    return [one, got[1], two, got[0], got[3], got[2]]


def wide_sum(arrays):
    total = arrays[0].astype(jnp.float32)
    for array in arrays[1:]:
        total = total + array.astype(jnp.float32)
    return total


def scatter_block(sums, half):
    one, two = sums[:2], sums[2:]
    got = together([("col", 1, two[1]), ("row", 1, one[1]), ("col", 3, two[3]), ("col", 2, two[2])])
    one = wide_sum([one[0], got[1]]).astype(jnp.bfloat16)
    two = wide_sum([two[0], got[0], got[3], got[2]]).astype(jnp.bfloat16)
    one = [one[half * n : half * (n + 1)] for n in range(4)]
    two = [two[half * n : half * (n + 1)] for n in range(2)]
    got = together([("col", 1, one[1]), ("row", 1, two[1]), ("col", 3, one[3]), ("col", 2, one[2])])
    return jnp.concatenate(
        [wide_sum([one[0], got[0], got[3], got[2]]), wide_sum([two[0], got[1]])], axis=0
    )


def norm_kernel(rows_ref, one_ref, two_ref):
    half = one_ref.shape[0]
    normed = layer_norm(rows_ref[...].astype(jnp.float32)).astype(jnp.bfloat16)
    one_ref[...] = normed[:half]
    two_ref[...] = normed[half:]


def norm(rows):
    part = jax.ShapeDtypeStruct((rows.shape[0] // 2, rows.shape[1]), jnp.bfloat16)
    return pl.pallas_call(
        norm_kernel,
        out_shape=(part, part),
        cost_estimate=pl.CostEstimate(
            flops=8 * rows.size, transcendentals=0, bytes_accessed=4 * rows.size
        ),
        name="norm",
    )(rows)


def mid_kernel(rows_ref, own_ref, a_ref, b_ref, c_ref, middle_ref, one_ref, two_ref):
    half = one_ref.shape[0]
    attention = wide_sum([own_ref[...], a_ref[...], b_ref[...], c_ref[...]])
    middle = (rows_ref[...].astype(jnp.float32) + attention).astype(jnp.bfloat16)
    middle_ref[...] = middle
    normed = layer_norm(middle.astype(jnp.float32)).astype(jnp.bfloat16)
    one_ref[...] = normed[:half]
    two_ref[...] = normed[half:]


def mid(rows, own, others):
    half, width = rows.shape[0] // 2, rows.shape[1]
    part = jax.ShapeDtypeStruct((half, width), jnp.bfloat16)
    return pl.pallas_call(
        mid_kernel,
        out_shape=(jax.ShapeDtypeStruct(rows.shape, jnp.bfloat16), part, part),
        cost_estimate=pl.CostEstimate(
            flops=12 * rows.size, transcendentals=0, bytes_accessed=14 * rows.size
        ),
        name="mid",
    )(rows, own, *others)


def joined_kernel(*refs):
    pieces, (heads_ref, out_ref, rows_ref) = refs[:8], refs[8:]
    tall = pieces[0].shape[0]
    for n in range(0, len(pieces), 4):
        for m in range(4):
            rows_ref[pl.ds(tall * m, tall), :] = pieces[n + m][...]
        out_ref[pl.ds(tall * n, 4 * tall), :] = jnp.dot(
            rows_ref[...], heads_ref[...], preferred_element_type=jnp.float32
        )


def join_heads(pieces, heads):
    tall, width = pieces[0].shape
    shape = (len(pieces) * tall, heads.shape[1])
    in_vmem = pl.BlockSpec(memory_space=pltpu.VMEM)
    return pl.pallas_call(
        joined_kernel,
        out_shape=jax.ShapeDtypeStruct(shape, jnp.float32),
        in_specs=[in_vmem] * (len(pieces) + 1),
        out_specs=in_vmem,
        scratch_shapes=[pltpu.VMEM((4 * tall, width), jnp.bfloat16)],
        compiler_params=pltpu.CompilerParams(vmem_limit_bytes=24 << 20),
        cost_estimate=pl.CostEstimate(
            flops=2 * shape[0] * width * shape[1], transcendentals=0, bytes_accessed=7 << 20
        ),
        name="join_heads",
    )(*pieces, heads)


def project_kernel(*refs):
    parts, fed_ref, outs = refs[:4], refs[4], refs[5:9]
    heads_ref, weight_ref, sems = refs[9:]
    shares = fed_ref.shape[0]
    tall = weight_ref.shape[0] // shares
    copies = [
        pltpu.make_async_copy(
            fed_ref.at[r, pl.ds(0, tall)], weight_ref.at[pl.ds(tall * r, tall)], sems.at[r]
        )
        for r in range(shares)
    ]
    for copy in copies:
        copy.start()
    size = parts[0].shape[1]
    for n, part in enumerate(parts):
        heads_ref[:, size * n : size * (n + 1)] = part[...]
    for copy in copies:
        copy.wait()
    step = 512

    @pl.loop(0, weight_ref.shape[1] // step)
    def _(j):
        span = pl.ds(pl.multiple_of(step * j, step), step)
        total = jnp.dot(
            heads_ref[...], weight_ref[:, span], preferred_element_type=jnp.float32
        ).astype(jnp.bfloat16)
        for n, out in enumerate(outs):
            out[:, span] = total[out.shape[0] * n : out.shape[0] * (n + 1)]


def project(parts, fed, local_rows):
    rows, size = parts[0].shape
    width = fed.shape[2]
    in_vmem = pl.BlockSpec(memory_space=pltpu.VMEM)
    return pl.pallas_call(
        project_kernel,
        out_shape=[jax.ShapeDtypeStruct((local_rows, width), jnp.bfloat16)] * 4,
        in_specs=[in_vmem] * 4 + [pl.BlockSpec(memory_space=pl.ANY)],
        out_specs=[in_vmem] * 4,
        scratch_shapes=[
            pltpu.VMEM((rows, 4 * size), jnp.bfloat16),
            pltpu.VMEM((4 * size, width), jnp.bfloat16),
            pltpu.SemaphoreType.DMA((fed.shape[0],)),
        ],
        cost_estimate=pl.CostEstimate(
            flops=8 * rows * size * width, transcendentals=0, bytes_accessed=4 << 20
        ),
        name="project",
    )(*parts, fed)


def feed_kernel(*refs):
    pieces, (w_in_ref, w_down_ref, fed_ref), outs = refs[:6], refs[6:9], refs[9:15]
    rows_ref, in_ref, down_ref, hidden_ref, sems = refs[15:]
    units, width = w_down_ref.shape
    shares, tall, _ = fed_ref.shape
    part_in, part_down = width // shares, units // shares
    first = tall - part_in // 2 - part_down
    half = width // 2
    jobs = [(w_in_ref, in_ref.at[0]), (w_down_ref, down_ref.at[0])]
    for r in range(shares):
        for n in range(2):
            jobs.append(
                (
                    fed_ref.at[r, pl.ds(first, part_in // 2), pl.ds(half * n, half)],
                    in_ref.at[1, pl.ds(part_in * r + part_in // 2 * n, part_in // 2)],
                )
            )
        jobs.append(
            (
                fed_ref.at[r, pl.ds(tall - part_down, part_down)],
                down_ref.at[1, pl.ds(part_down * r, part_down)],
            )
        )
    copies = [
        pltpu.make_async_copy(source, target, sems.at[n])
        for n, (source, target) in enumerate(jobs)
    ]
    for copy in copies:
        copy.start()
    at = 0
    for piece in pieces:
        rows_ref[pl.ds(at, piece.shape[0]), :] = piece[...]
        at += piece.shape[0]
    copies[0].wait()
    step = 256
    for shard in range(2):
        if shard == 1:
            for copy in copies[1:]:
                copy.wait()

        @pl.loop(0, units // step)
        def _(j):
            at = pl.multiple_of(step * j, step)
            gate = jnp.dot(
                rows_ref[...],
                in_ref[shard, :, pl.ds(at, step)],
                preferred_element_type=jnp.float32,
            )
            up = jnp.dot(
                rows_ref[...],
                in_ref[shard, :, pl.ds(pl.multiple_of(units + at, step), step)],
                preferred_element_type=jnp.float32,
            )
            hidden = gate / (1.0 + jnp.exp(-gate)) * up
            hidden_ref[shard, :, pl.ds(at, step)] = hidden.astype(jnp.bfloat16)

    @pl.loop(0, width // step)
    def _(j):
        span = pl.ds(pl.multiple_of(step * j, step), step)
        total = jnp.dot(
            hidden_ref[0], down_ref[0, :, span], preferred_element_type=jnp.float32
        ) + jnp.dot(hidden_ref[1], down_ref[1, :, span], preferred_element_type=jnp.float32)
        total = total.astype(jnp.bfloat16)
        at = 0
        for out in outs:
            out[:, span] = total[at : at + out.shape[0]]
            at += out.shape[0]


def feed(pieces, w_in, w_down, fed):
    units, width = w_down.shape
    rows = sum(piece.shape[0] for piece in pieces)
    return pl.pallas_call(
        feed_kernel,
        out_shape=[jax.ShapeDtypeStruct(piece.shape, jnp.bfloat16) for piece in pieces],
        in_specs=[pl.BlockSpec(memory_space=pltpu.VMEM)] * len(pieces)
        + [pl.BlockSpec(memory_space=pl.ANY)] * 3,
        out_specs=[pl.BlockSpec(memory_space=pltpu.VMEM)] * len(pieces),
        scratch_shapes=[
            pltpu.VMEM((rows, width), jnp.bfloat16),
            pltpu.VMEM((2, width, 2 * units), jnp.bfloat16),
            pltpu.VMEM((2, units, width), jnp.bfloat16),
            pltpu.VMEM((2, rows, units), jnp.bfloat16),
            pltpu.SemaphoreType.DMA((2 + 3 * fed.shape[0],)),
        ],
        compiler_params=pltpu.CompilerParams(vmem_limit_bytes=48 << 20),
        cost_estimate=pl.CostEstimate(
            flops=12 * rows * width * units, transcendentals=2 * rows * units,
            bytes_accessed=16 << 20,
        ),
        name="feed",
    )(*pieces, w_in, w_down, fed)


def attend_kernel(
    place_ref, length_ref, span_ref, target_ref,
    joined_ref, cache_ref, cos_ref, sin_ref, far_cos_ref, far_sin_ref, context_ref, new_ref,
):
    g = pl.program_id(0)
    row, column = place_ref[0], place_ref[1]
    request = request_of(g, row)
    length_old = length_ref[request]
    away = row ^ (request // 2)
    columns = [column ^ (2 * (request % 2) + n) for n in range(2)]

    def block(n):
        return joined_ref[pl.ds(pl.multiple_of(32 * n, 32), 32), :]

    joined = jnp.concatenate(
        [block(n) for c in columns for n in (4 * away + c, 16 + 4 * c + away)], axis=0
    )
    far_cos, far_sin = far_cos_ref[pl.ds(request, 1), :], far_sin_ref[pl.ds(request, 1), :]
    cosine = far_cos * cos_ref[...] - far_sin * sin_ref[...]
    sine = far_sin * cos_ref[...] + far_cos * sin_ref[...]

    def turned(part):
        return (part * cosine + pltpu.roll(part, 64, axis=1) * sine).astype(jnp.bfloat16)

    queries = turned(joined[:, :128])
    keys_new = turned(joined[:, 128:256])
    values_new = joined[:, 256:].astype(jnp.bfloat16)
    stored = cache_ref.shape[2]
    whole = new_ref.shape[2]
    live = lax.broadcasted_iota(jnp.int32, keys_new.shape, 0) < span_ref[request]
    rows = lax.broadcasted_iota(jnp.int32, (whole, keys_new.shape[1]), 0)
    for kind, fresh in enumerate((keys_new, values_new)):
        fresh = jnp.where(live, fresh.astype(jnp.float32), 0.0)
        fresh = jnp.concatenate(
            [fresh, jnp.zeros((whole - fresh.shape[0], fresh.shape[1]), jnp.float32)], axis=0
        )
        old = cache_ref[0, kind].astype(jnp.float32)
        old = jnp.concatenate(
            [old, jnp.zeros((whole - stored, old.shape[1]), jnp.float32)], axis=0
        )
        fresh = pltpu.roll(fresh, length_old, axis=0)
        new_ref[0, kind] = jnp.where(rows < length_old, old, fresh).astype(jnp.bfloat16)
    scale = 1.0 / math.sqrt(128)
    contract = (((1,), (1,)), ((), ()))
    old = (
        lax.dot_general(queries, cache_ref[0, 0], contract, preferred_element_type=jnp.float32)
        * scale
    )
    new = (
        lax.dot_general(queries, keys_new, contract, preferred_element_type=jnp.float32) * scale
    )
    old_ok = lax.broadcasted_iota(jnp.int32, old.shape, 1) < length_old
    new_ok = lax.broadcasted_iota(jnp.int32, new.shape, 1) <= lax.broadcasted_iota(
        jnp.int32, new.shape, 0
    )
    old = jnp.where(old_ok, old, -1e30)
    new = jnp.where(new_ok, new, -1e30)
    highest = jnp.maximum(
        jnp.max(old, axis=1, keepdims=True), jnp.max(new, axis=1, keepdims=True)
    )
    old = jnp.where(old_ok, jnp.exp(old - highest), 0.0)
    new = jnp.where(new_ok, jnp.exp(new - highest), 0.0)
    total = jnp.sum(old, axis=1, keepdims=True) + jnp.sum(new, axis=1, keepdims=True)
    old_weights = (old / total).astype(jnp.bfloat16)
    new_weights = (new / total).astype(jnp.bfloat16)
    stored_values = cache_ref[0, 1]
    context = jnp.dot(
        old_weights, stored_values, preferred_element_type=jnp.float32
    ) + jnp.dot(new_weights, values_new, preferred_element_type=jnp.float32)
    context = context.astype(jnp.bfloat16)
    for n in range(2):
        place = pl.multiple_of(64 * (4 * (g // 2) + columns[n]), 64)
        context_ref[pl.ds(place, 64), :] = context[64 * n : 64 * n + 64]


def request_of(g, row):
    return 2 * (row ^ (g // 2)) + g % 2


def attend(place, lengths, spans, targets, joined, cache, tables, replicas):
    slots, kinds, stored, size = cache.shape
    span = tables[0].shape[0]
    whole = lambda g, *refs: (0, 0)
    return pl.pallas_call(
        attend_kernel,
        out_shape=(
            jax.ShapeDtypeStruct((slots * span, size), jnp.bfloat16),
            jax.ShapeDtypeStruct((replicas, kinds, stored + span, size), jnp.bfloat16),
        ),
        grid_spec=pltpu.PrefetchScalarGridSpec(
            num_scalar_prefetch=4,
            grid=(slots,),
            in_specs=[
                pl.BlockSpec(memory_space=pltpu.VMEM),
                pl.BlockSpec(
                    (1, kinds, stored, size),
                    lambda g, place, *refs: (request_of(g, place[0]), 0, 0, 0),
                ),
            ]
            + [pl.BlockSpec(table.shape, whole) for table in tables],
            out_specs=[
                pl.BlockSpec((slots * span, size), whole),
                pl.BlockSpec(
                    (1, kinds, stored + span, size),
                    lambda g, place, lengths, spans, targets: (
                        targets[request_of(g, place[0])], 0, 0, 0,
                    ),
                ),
            ],
        ),
        cost_estimate=pl.CostEstimate(
            flops=4 * slots * span * (stored + span) * size,
            transcendentals=slots * span * (stored + span),
            bytes_accessed=6 << 20,
        ),
        name="attend",
    )(place, lengths, spans, targets, joined, cache, *tables)


def pick_kernel(source_ref, moved_ref, out_ref, held_ref, sems):
    slots = out_ref.shape[0]
    taken = [
        pltpu.make_async_copy(moved_ref.at[source_ref[t]], held_ref.at[t], sems.at[0, t])
        for t in range(slots)
    ]
    given = [
        pltpu.make_async_copy(held_ref.at[t], out_ref.at[t], sems.at[1, t]) for t in range(slots)
    ]
    for copy in taken:
        copy.start()
    for t in range(slots):
        taken[t].wait()
        given[t].start()
    for copy in given:
        copy.wait()


def pick(moved, source):
    shape = (source.shape[0],) + moved.shape[1:]
    return pl.pallas_call(
        pick_kernel,
        out_shape=jax.ShapeDtypeStruct(shape, moved.dtype),
        in_specs=[pl.BlockSpec(memory_space=pltpu.SMEM), pl.BlockSpec(memory_space=pl.ANY)],
        out_specs=pl.BlockSpec(memory_space=pl.ANY),
        scratch_shapes=[pltpu.VMEM(shape, moved.dtype), pltpu.SemaphoreType.DMA((2, shape[0]))],
        cost_estimate=pl.CostEstimate(
            flops=0, transcendentals=0, bytes_accessed=4 * math.prod(shape)
        ),
        name="pick",
    )(source, moved)


def body(hidden_in, w_qkv, w_out, w_gate_up, w_down, cache, span_len, cache_len, new_slot):
    slots, kinds, stored, _, size = cache.shape
    local_rows, width = hidden_in.shape
    units = w_down.shape[0]
    span = 16 * local_rows // slots
    replica = lax.axis_index("rep")
    replicas = lax.axis_size("rep")
    row, column = lax.axis_index("row"), lax.axis_index("col")
    cache = cache.reshape(slots, kinds, stored, size)
    lengths = lax.dynamic_slice_in_dim(cache_len, replica * slots, slots)
    spans = lax.dynamic_slice_in_dim(span_len, replica * slots, slots)
    targets = lax.dynamic_slice_in_dim(new_slot, replica * slots, slots) // slots
    my_slots = replica * slots + jnp.arange(slots, dtype=jnp.int32)
    arrivals = (new_slot[None, :] == my_slots[:, None]).astype(jnp.int32)
    requests = jnp.arange(new_slot.shape[0], dtype=jnp.int32)
    source = jnp.sum(arrivals * (requests // slots)[None, :], axis=1)

    one, two = norm(hidden_in)
    one, two, w_gate_up = lax.optimization_barrier((one, two, w_gate_up))

    out_rows = 4 * size // replicas
    out_slice = lax.dynamic_slice_in_dim(
        w_out.reshape(size, width), out_rows * (replica % (size // out_rows)), out_rows
    )
    per_head = size // out_rows
    pairs = [
        (4 * r + i, 4 * r + (i ^ (r // per_head))) for r in range(replicas) for i in range(4)
    ]
    out_far = lax.ppermute(out_slice, ("rep", "row"), pairs)
    rows_in, rows_down = width // replicas, units // replicas
    in_slice = lax.dynamic_slice_in_dim(w_gate_up, replica * rows_in, rows_in)
    in_slice = in_slice.reshape(2, rows_in // 2, 2 * units)
    down_slice = lax.dynamic_slice_in_dim(w_down, replica * rows_down, rows_down)
    feed_slice = jnp.concatenate(
        [jnp.concatenate([in_slice[0], in_slice[1]], axis=1), down_slice], axis=0
    )
    feed_far = swap("row", 2, feed_slice)

    pieces, (out_far, feed_far) = gather_plane(one, two, [out_far, feed_far])
    fed = lax.all_gather(
        jnp.concatenate([out_far, feed_far], axis=0), "rep", axis=0, tiled=False
    )
    w_in = w_gate_up.reshape(width, 2 * units)
    pieces, w_in = lax.optimization_barrier((pieces, w_in))
    joined = join_heads(pieces, w_qkv.reshape(width, 3 * size))

    frequency = 10000.0 ** (-(np.arange(size // 2) * 2.0 / size))
    frequency = np.concatenate([frequency, frequency])[None, :]
    sign = np.where(np.arange(size) < size // 2, -1.0, 1.0)[None, :]
    near = np.arange(span)[:, None] * frequency
    far = lengths.astype(jnp.float32)[:, None] * jnp.asarray(frequency, jnp.float32)
    tables = (
        jnp.asarray(np.cos(near), jnp.float32),
        jnp.asarray(np.sin(near) * sign, jnp.float32),
        jnp.cos(far),
        jnp.sin(far) * jnp.asarray(sign, jnp.float32),
    )
    place = jnp.stack([row, column]).astype(jnp.int32)
    context, sent = attend(place, lengths, spans, targets, joined, cache, tables, replicas)

    context = context.reshape(4, 4 * local_rows, size)
    got = together([("row", k, context[k]) for k in (1, 3, 2)])
    partial = project([context[0], got[0], got[2], got[1]], fed, local_rows)
    partial, sent = lax.optimization_barrier((partial, sent))
    got = together([("col", k, partial[k]) for k in (1, 3, 2)])
    middle, one, two = mid(hidden_in, partial[0], [got[0], got[2], got[1]])
    moved = lax.all_to_all(sent, "rep", split_axis=0, concat_axis=0, tiled=True)
    sums = feed(gather_block(one, two), w_in, w_down, fed)
    down_sum = scatter_block(sums, local_rows // 2)

    cache_out = pick(moved, source)
    first_row = (row * 4 + column) * local_rows
    within = first_row % span + jnp.arange(local_rows, dtype=jnp.int32)
    live = within < lax.dynamic_index_in_dim(spans, first_row // span, keepdims=False)
    hidden_out = jnp.where(live[:, None], middle.astype(jnp.float32) + down_sum, 0.0)
    return (
        hidden_out.astype(jnp.bfloat16),
        cache_out.reshape(slots, kinds, stored + span, 1, size),
    )


def solution(mesh):
    in_specs = (
        P(("rep", "row", "col"), None),
        P(None, ("row", "col"), None),
        P(("row", "col"), None, None),
        P(None, None, ("row", "col")),
        P(("row", "col"), None),
        P("rep", None, None, ("row", "col"), None),
        P(),
        P(),
        P(),
    )
    out_specs = (P(("rep", "row", "col"), None), P("rep", None, None, ("row", "col"), None))
    return jax.shard_map(body, mesh=mesh, in_specs=in_specs, out_specs=out_specs, check_vma=False)
```

```python
import math

import jax
import jax.numpy as jnp
import numpy as np
from jax import lax
from jax.experimental import pallas as pl
from jax.experimental.pallas import tpu as pltpu
from jax.sharding import PartitionSpec as P

EPSILON = 1e-05


def layer_norm(values):
    centred = values - jnp.mean(values, axis=-1, keepdims=True)
    spread = jnp.mean(centred * centred, axis=-1, keepdims=True)
    return centred * lax.rsqrt(spread + EPSILON)


def swap(axis, k, array):
    size = lax.axis_size(axis)
    return lax.ppermute(array, axis, [(i, i ^ k) for i in range(size)])


def together(sent):
    got = [swap(axis, k, array) for axis, k, array in sent]
    return lax.optimization_barrier(got)


def join(pieces):
    return lax.optimization_barrier(jnp.concatenate(pieces, axis=0))


def gather_plane(one, two, two_more, also):
    sent = [("col", 1, one), ("row", 1, two), ("col", 3, one), ("row", 3, two)]
    sent += [("col", 2, one), ("row", 2, two_more)]
    got = lax.optimization_barrier([swap(*x) for x in sent] + [also])
    tall = two.shape[0]
    more = [got[6], got[5][tall:]]
    one = join([one, got[0], got[4], got[2]])
    two = join([two, got[1], got[5][:tall], got[3]])
    got = together([x for k in (1, 3, 2) for x in (("row", k, one), ("col", k, two))])
    return [one, got[0], got[4], got[2], two, got[1], got[5], got[3]], more


def gather_block(one, two):
    got = together([("col", 1, one), ("row", 1, two), ("col", 3, one), ("col", 2, one)])
    two = join([two, got[1]])
    one = join([one, got[0], got[3], got[2]])
    got = together([("col", 1, two), ("row", 1, one), ("col", 3, two), ("col", 2, two)])
    return [one, got[1], two, got[0], got[3], got[2]]


def wide_sum(arrays):
    total = arrays[0].astype(jnp.float32)
    for array in arrays[1:]:
        total = total + array.astype(jnp.float32)
    return total


def scatter_block(sums, half):
    one, two = sums[:2], sums[2:]
    got = together([("col", 1, two[1]), ("row", 1, one[1]), ("col", 3, two[3]), ("col", 2, two[2])])
    one = wide_sum([one[0], got[1]]).astype(jnp.bfloat16)
    two = wide_sum([two[0], got[0], got[3], got[2]]).astype(jnp.bfloat16)
    one = [one[half * n : half * (n + 1)] for n in range(4)]
    two = [two[half * n : half * (n + 1)] for n in range(2)]
    got = together([("col", 1, one[1]), ("row", 1, two[1]), ("col", 3, one[3]), ("col", 2, one[2])])
    return jnp.concatenate(
        [wide_sum([one[0], got[0], got[3], got[2]]), wide_sum([two[0], got[1]])], axis=0
    )


def norm_kernel(rows_ref, one_ref, two_ref):
    half = one_ref.shape[0]
    normed = layer_norm(rows_ref[...].astype(jnp.float32)).astype(jnp.bfloat16)
    one_ref[...] = normed[:half]
    two_ref[...] = normed[half:]


def norm(rows):
    part = jax.ShapeDtypeStruct((rows.shape[0] // 2, rows.shape[1]), jnp.bfloat16)
    return pl.pallas_call(
        norm_kernel,
        out_shape=(part, part),
        compiler_params=pltpu.CompilerParams(vmem_limit_bytes=4 << 20),
        cost_estimate=pl.CostEstimate(
            flops=8 * rows.size, transcendentals=0, bytes_accessed=4 * rows.size
        ),
        name="norm",
    )(rows)


def mid_kernel(rows_ref, own_ref, a_ref, b_ref, c_ref, middle_ref, one_ref, two_ref):
    half = one_ref.shape[0]
    attention = wide_sum([own_ref[...], a_ref[...], b_ref[...], c_ref[...]])
    middle = (rows_ref[...].astype(jnp.float32) + attention).astype(jnp.bfloat16)
    middle_ref[...] = middle
    normed = layer_norm(middle.astype(jnp.float32)).astype(jnp.bfloat16)
    one_ref[...] = normed[:half]
    two_ref[...] = normed[half:]


def mid(rows, own, others):
    half, width = rows.shape[0] // 2, rows.shape[1]
    part = jax.ShapeDtypeStruct((half, width), jnp.bfloat16)
    return pl.pallas_call(
        mid_kernel,
        out_shape=(jax.ShapeDtypeStruct(rows.shape, jnp.bfloat16), part, part),
        compiler_params=pltpu.CompilerParams(vmem_limit_bytes=6 << 20),
        cost_estimate=pl.CostEstimate(
            flops=12 * rows.size, transcendentals=0, bytes_accessed=14 * rows.size
        ),
        name="mid",
    )(rows, own, *others)


def joined_kernel(*refs):
    pieces, (heads_ref, out_ref, rows_ref) = refs[:8], refs[8:]
    tall = pieces[0].shape[0]
    for n in range(0, len(pieces), 4):
        for m in range(4):
            rows_ref[pl.ds(tall * m, tall), :] = pieces[n + m][...]
        out_ref[pl.ds(tall * n, 4 * tall), :] = jnp.dot(
            rows_ref[...], heads_ref[...], preferred_element_type=jnp.float32
        )


def join_heads(pieces, heads):
    tall, width = pieces[0].shape
    shape = (len(pieces) * tall, heads.shape[1])
    in_vmem = pl.BlockSpec(memory_space=pltpu.VMEM)
    return pl.pallas_call(
        joined_kernel,
        out_shape=jax.ShapeDtypeStruct(shape, jnp.float32),
        in_specs=[in_vmem] * (len(pieces) + 1),
        out_specs=in_vmem,
        scratch_shapes=[pltpu.VMEM((4 * tall, width), jnp.bfloat16)],
        compiler_params=pltpu.CompilerParams(vmem_limit_bytes=10 << 20),
        cost_estimate=pl.CostEstimate(
            flops=2 * shape[0] * width * shape[1], transcendentals=0, bytes_accessed=7 << 20
        ),
        name="join_heads",
    )(*pieces, heads)


def project_kernel(*refs):
    parts, fed_ref, outs = refs[:4], refs[4], refs[5:9]
    heads_ref, weight_ref, sems = refs[9:]
    shares = fed_ref.shape[0]
    tall = weight_ref.shape[0] // shares
    copies = [
        pltpu.make_async_copy(
            fed_ref.at[r, pl.ds(0, tall)], weight_ref.at[pl.ds(tall * r, tall)], sems.at[r]
        )
        for r in range(shares)
    ]
    for copy in copies:
        copy.start()
    size = parts[0].shape[1]
    for n, part in enumerate(parts):
        heads_ref[:, size * n : size * (n + 1)] = part[...]
    for copy in copies:
        copy.wait()
    step = 512

    @pl.loop(0, weight_ref.shape[1] // step)
    def _(j):
        span = pl.ds(pl.multiple_of(step * j, step), step)
        total = jnp.dot(
            heads_ref[...], weight_ref[:, span], preferred_element_type=jnp.float32
        ).astype(jnp.bfloat16)
        for n, out in enumerate(outs):
            out[:, span] = total[out.shape[0] * n : out.shape[0] * (n + 1)]


def project(parts, fed, local_rows):
    rows, size = parts[0].shape
    width = fed.shape[2]
    in_vmem = pl.BlockSpec(memory_space=pltpu.VMEM)
    return pl.pallas_call(
        project_kernel,
        out_shape=[jax.ShapeDtypeStruct((local_rows, width), jnp.bfloat16)] * 4,
        in_specs=[in_vmem] * 4 + [pl.BlockSpec(memory_space=pltpu.HBM)],
        out_specs=[in_vmem] * 4,
        scratch_shapes=[
            pltpu.VMEM((rows, 4 * size), jnp.bfloat16),
            pltpu.VMEM((4 * size, width), jnp.bfloat16),
            pltpu.SemaphoreType.DMA((fed.shape[0],)),
        ],
        compiler_params=pltpu.CompilerParams(vmem_limit_bytes=10 << 20),
        cost_estimate=pl.CostEstimate(
            flops=8 * rows * size * width, transcendentals=0, bytes_accessed=4 << 20
        ),
        name="project",
    )(*parts, fed)


def feed_kernel(*refs):
    pieces, (w_in_ref, w_down_ref, fed_ref), outs = refs[:6], refs[6:9], refs[9:15]
    rows_ref, in_ref, down_ref, hidden_ref, sems = refs[15:]
    units, width = w_down_ref.shape
    shares, tall, _ = fed_ref.shape
    part_in, part_down = width // shares, units // shares
    first = tall - part_in // 2 - part_down
    half = width // 2
    jobs = []
    for r in range(shares):
        for n in range(2):
            jobs.append(
                (
                    fed_ref.at[r, pl.ds(first, part_in // 2), pl.ds(half * n, half)],
                    in_ref.at[pl.ds(part_in * r + part_in // 2 * n, part_in // 2)],
                )
            )
        jobs.append(
            (
                fed_ref.at[r, pl.ds(tall - part_down, part_down)],
                down_ref.at[pl.ds(part_down * r, part_down)],
            )
        )
    copies = [
        pltpu.make_async_copy(source, target, sems.at[n])
        for n, (source, target) in enumerate(jobs)
    ]
    for copy in copies:
        copy.start()
    at = 0
    for piece in pieces:
        rows_ref[pl.ds(at, piece.shape[0]), :] = piece[...]
        at += piece.shape[0]
    step = 256
    for shard, weight_ref in enumerate((w_in_ref, in_ref)):
        if shard == 1:
            for copy in copies:
                copy.wait()

        @pl.loop(0, units // step)
        def _(j):
            at = pl.multiple_of(step * j, step)
            gate = jnp.dot(
                rows_ref[...],
                weight_ref[:, pl.ds(at, step)],
                preferred_element_type=jnp.float32,
            )
            up = jnp.dot(
                rows_ref[...],
                weight_ref[:, pl.ds(pl.multiple_of(units + at, step), step)],
                preferred_element_type=jnp.float32,
            )
            hidden = gate / (1.0 + jnp.exp(-gate)) * up
            hidden_ref[shard, :, pl.ds(at, step)] = hidden.astype(jnp.bfloat16)

    @pl.loop(0, width // step)
    def _(j):
        span = pl.ds(pl.multiple_of(step * j, step), step)
        total = jnp.dot(
            hidden_ref[0], w_down_ref[:, span], preferred_element_type=jnp.float32
        ) + jnp.dot(hidden_ref[1], down_ref[:, span], preferred_element_type=jnp.float32)
        total = total.astype(jnp.bfloat16)
        at = 0
        for out in outs:
            out[:, span] = total[at : at + out.shape[0]]
            at += out.shape[0]


def feed(pieces, w_in, w_down, fed):
    units, width = w_down.shape
    rows = sum(piece.shape[0] for piece in pieces)
    return pl.pallas_call(
        feed_kernel,
        out_shape=[jax.ShapeDtypeStruct(piece.shape, jnp.bfloat16) for piece in pieces],
        in_specs=[pl.BlockSpec(memory_space=pltpu.VMEM)] * (len(pieces) + 2)
        + [pl.BlockSpec(memory_space=pltpu.HBM)],
        out_specs=[pl.BlockSpec(memory_space=pltpu.VMEM)] * len(pieces),
        scratch_shapes=[
            pltpu.VMEM((rows, width), jnp.bfloat16),
            pltpu.VMEM((width, 2 * units), jnp.bfloat16),
            pltpu.VMEM((units, width), jnp.bfloat16),
            pltpu.VMEM((2, rows, units), jnp.bfloat16),
            pltpu.SemaphoreType.DMA((3 * fed.shape[0],)),
        ],
        compiler_params=pltpu.CompilerParams(vmem_limit_bytes=18 << 20),
        cost_estimate=pl.CostEstimate(
            flops=12 * rows * width * units, transcendentals=2 * rows * units,
            bytes_accessed=16 << 20,
        ),
        name="feed",
    )(*pieces, w_in, w_down, fed)


def attend_one(
    request, away, column, length_old, span_new,
    joined_ref, cache_ref, cos_ref, sin_ref, far_cos_ref, far_sin_ref, new_ref,
):
    columns = [column ^ (2 * (request % 2) + n) for n in range(2)]

    def block(n):
        return joined_ref[pl.ds(pl.multiple_of(32 * n, 32), 32), :]

    joined = jnp.concatenate(
        [block(n) for c in columns for n in (4 * away + c, 16 + 4 * c + away)], axis=0
    )
    far_cos, far_sin = far_cos_ref[pl.ds(request, 1), :], far_sin_ref[pl.ds(request, 1), :]
    cosine = far_cos * cos_ref[...] - far_sin * sin_ref[...]
    sine = far_sin * cos_ref[...] + far_cos * sin_ref[...]

    def turned(part):
        return (part * cosine + pltpu.roll(part, 64, axis=1) * sine).astype(jnp.bfloat16)

    queries = turned(joined[:, :128])
    keys_new = turned(joined[:, 128:256])
    values_new = joined[:, 256:].astype(jnp.bfloat16)
    stored, whole = cache_ref.shape[1], new_ref.shape[1]
    live = lax.broadcasted_iota(jnp.int32, keys_new.shape, 0) < span_new
    rows = lax.broadcasted_iota(jnp.int32, (whole, keys_new.shape[1]), 0)
    for kind, fresh in enumerate((keys_new, values_new)):
        fresh = jnp.where(live, fresh.astype(jnp.float32), 0.0)
        fresh = jnp.concatenate(
            [fresh, jnp.zeros((whole - fresh.shape[0], fresh.shape[1]), jnp.float32)], axis=0
        )
        old = cache_ref[kind].astype(jnp.float32)
        old = jnp.concatenate(
            [old, jnp.zeros((whole - stored, old.shape[1]), jnp.float32)], axis=0
        )
        fresh = pltpu.roll(fresh, length_old, axis=0)
        new_ref[kind] = jnp.where(rows < length_old, old, fresh).astype(jnp.bfloat16)
    scale = 1.0 / math.sqrt(128)
    contract = (((1,), (1,)), ((), ()))
    old = (
        lax.dot_general(queries, cache_ref[0], contract, preferred_element_type=jnp.float32)
        * scale
    )
    new = (
        lax.dot_general(queries, keys_new, contract, preferred_element_type=jnp.float32) * scale
    )
    old_ok = lax.broadcasted_iota(jnp.int32, old.shape, 1) < length_old
    new_ok = lax.broadcasted_iota(jnp.int32, new.shape, 1) <= lax.broadcasted_iota(
        jnp.int32, new.shape, 0
    )
    old = jnp.where(old_ok, old, -1e30)
    new = jnp.where(new_ok, new, -1e30)
    highest = jnp.maximum(
        jnp.max(old, axis=1, keepdims=True), jnp.max(new, axis=1, keepdims=True)
    )
    old = jnp.where(old_ok, jnp.exp(old - highest), 0.0)
    new = jnp.where(new_ok, jnp.exp(new - highest), 0.0)
    total = jnp.sum(old, axis=1, keepdims=True) + jnp.sum(new, axis=1, keepdims=True)
    context = jnp.dot(
        (old / total).astype(jnp.bfloat16), cache_ref[1], preferred_element_type=jnp.float32
    ) + jnp.dot(
        (new / total).astype(jnp.bfloat16), values_new, preferred_element_type=jnp.float32
    )
    return context.astype(jnp.bfloat16), columns


def attend_kernel(
    place_ref, length_ref, span_ref, target_ref,
    joined_ref, cache_ref, cos_ref, sin_ref, far_cos_ref, far_sin_ref, *refs,
):
    contexts, (sent_ref, held_ref, sems) = refs[:4], refs[4:]
    step = pl.program_id(0)
    column = place_ref[1]
    source_row = place_ref[0] ^ step

    def copy_of(n, target):
        return pltpu.make_async_copy(held_ref.at[n], sent_ref.at[target], sems.at[n])

    for m in range(2):
        request = 2 * source_row + m
        context, columns = attend_one(
            request, step, column, length_ref[request], span_ref[request],
            joined_ref, cache_ref.at[m], cos_ref, sin_ref, far_cos_ref, far_sin_ref,
            held_ref.at[2 * step + m],
        )
        for n in range(2):
            for q in range(4):

                @pl.when(step == q)
                def _():
                    at = pl.multiple_of(64 * columns[n], 64)
                    contexts[q][pl.ds(at, 64), :] = context[64 * n : 64 * n + 64]

        copy_of(2 * step + m, target_ref[request]).start()

    @pl.when(step == 3)
    def _():
        for n in range(8):
            copy_of(n, target_ref[2 * (place_ref[0] ^ (n // 2)) + n % 2]).wait()


def attend(place, lengths, spans, targets, joined, cache, tables, replicas):
    slots, kinds, stored, size = cache.shape
    span = tables[0].shape[0]
    in_vmem = pl.BlockSpec(memory_space=pltpu.VMEM)
    context = jax.ShapeDtypeStruct((slots // 4 * span, size), jnp.bfloat16)
    return pl.pallas_call(
        attend_kernel,
        out_shape=[context] * 4
        + [pltpu.HBM((replicas, kinds, stored + span, size), jnp.bfloat16)],
        grid_spec=pltpu.PrefetchScalarGridSpec(
            num_scalar_prefetch=4,
            grid=(4,),
            in_specs=[
                in_vmem,
                pl.BlockSpec(
                    (slots // 4, kinds, stored, size),
                    lambda step, place, *refs: (place[0] ^ step, 0, 0, 0),
                ),
            ]
            + [in_vmem] * len(tables),
            out_specs=[in_vmem] * 4 + [pl.BlockSpec(memory_space=pltpu.HBM)],
            scratch_shapes=[
                pltpu.VMEM((slots, kinds, stored + span, size), jnp.bfloat16),
                pltpu.SemaphoreType.DMA((slots,)),
            ],
        ),
        compiler_params=pltpu.CompilerParams(vmem_limit_bytes=12 << 20),
        cost_estimate=pl.CostEstimate(
            flops=4 * slots * span * (stored + span) * size,
            transcendentals=slots * span * (stored + span),
            bytes_accessed=6 << 20,
        ),
        name="attend",
    )(place, lengths, spans, targets, joined, cache, *tables)


def pick_kernel(source_ref, moved_ref, out_ref, held_ref, sems):
    slots = out_ref.shape[0]
    taken = [
        pltpu.make_async_copy(moved_ref.at[source_ref[t]], held_ref.at[t], sems.at[0, t])
        for t in range(slots)
    ]
    given = [
        pltpu.make_async_copy(held_ref.at[t], out_ref.at[t], sems.at[1, t]) for t in range(slots)
    ]
    for copy in taken:
        copy.start()
    for t in range(slots):
        taken[t].wait()
        given[t].start()
    for copy in given:
        copy.wait()


def pick(moved, source):
    shape = (source.shape[0],) + moved.shape[1:]
    return pl.pallas_call(
        pick_kernel,
        out_shape=jax.ShapeDtypeStruct(shape, moved.dtype),
        in_specs=[pl.BlockSpec(memory_space=pltpu.SMEM), pl.BlockSpec(memory_space=pltpu.HBM)],
        out_specs=pl.BlockSpec(memory_space=pltpu.HBM),
        scratch_shapes=[pltpu.VMEM(shape, moved.dtype), pltpu.SemaphoreType.DMA((2, shape[0]))],
        cost_estimate=pl.CostEstimate(
            flops=0, transcendentals=0, bytes_accessed=4 * math.prod(shape)
        ),
        name="pick",
    )(source, moved)


def body(hidden_in, w_qkv, w_out, w_gate_up, w_down, cache, span_len, cache_len, new_slot):
    slots, kinds, stored, _, size = cache.shape
    local_rows, width = hidden_in.shape
    units = w_down.shape[0]
    span = 16 * local_rows // slots
    replica = lax.axis_index("rep")
    replicas = lax.axis_size("rep")
    row, column = lax.axis_index("row"), lax.axis_index("col")
    cache = cache.reshape(slots, kinds, stored, size)
    lengths = lax.dynamic_slice_in_dim(cache_len, replica * slots, slots)
    spans = lax.dynamic_slice_in_dim(span_len, replica * slots, slots)
    targets = lax.dynamic_slice_in_dim(new_slot, replica * slots, slots) // slots
    my_slots = replica * slots + jnp.arange(slots, dtype=jnp.int32)
    arrivals = (new_slot[None, :] == my_slots[:, None]).astype(jnp.int32)
    requests = jnp.arange(new_slot.shape[0], dtype=jnp.int32)
    source = jnp.sum(arrivals * (requests // slots)[None, :], axis=1)

    one, two = norm(hidden_in)
    one, two, w_gate_up = lax.optimization_barrier((one, two, w_gate_up))

    out_rows = 4 * size // replicas
    out_slice = lax.dynamic_slice_in_dim(
        w_out.reshape(size, width), out_rows * (replica % (size // out_rows)), out_rows
    )
    per_head = size // out_rows
    pairs = [
        (4 * r + i, 4 * r + (i ^ (r // per_head))) for r in range(replicas) for i in range(4)
    ]
    out_far = lax.ppermute(out_slice, ("rep", "row"), pairs)
    rows_in, rows_down = width // replicas, units // replicas
    in_slice = lax.dynamic_slice_in_dim(w_gate_up, replica * rows_in, rows_in)
    in_slice = in_slice.reshape(2, rows_in // 2, 2 * units)
    down_slice = lax.dynamic_slice_in_dim(w_down, replica * rows_down, rows_down)
    two_more = jnp.concatenate(
        [two, jnp.concatenate([in_slice[0], in_slice[1]], axis=1), down_slice], axis=0
    )

    pieces, more = gather_plane(one, two, two_more, out_far)
    fed = lax.all_gather(
        jnp.concatenate(more, axis=0), "rep", axis=0, tiled=False
    )
    w_in = w_gate_up.reshape(width, 2 * units)
    pieces, w_in = lax.optimization_barrier((pieces, w_in))
    joined = join_heads(pieces, w_qkv.reshape(width, 3 * size))

    frequency = 10000.0 ** (-(np.arange(size // 2) * 2.0 / size))
    frequency = np.concatenate([frequency, frequency])[None, :]
    sign = np.where(np.arange(size) < size // 2, -1.0, 1.0)[None, :]
    near = np.arange(span)[:, None] * frequency
    far = lengths.astype(jnp.float32)[:, None] * jnp.asarray(frequency, jnp.float32)
    tables = (
        jnp.asarray(np.cos(near), jnp.float32),
        jnp.asarray(np.sin(near) * sign, jnp.float32),
        jnp.cos(far),
        jnp.sin(far) * jnp.asarray(sign, jnp.float32),
    )
    place = jnp.stack([row, column]).astype(jnp.int32)
    *context, sent = attend(place, lengths, spans, targets, joined, cache, tables, replicas)

    got, sent = lax.optimization_barrier(([swap("row", k, context[k]) for k in (1, 3, 2)], sent))
    fed = pltpu.with_memory_space_constraint(fed, pltpu.HBM)
    partial = project([context[0], got[0], got[2], got[1]], fed, local_rows)
    got = together([("col", k, partial[k]) for k in (1, 3, 2)])
    middle, one, two = mid(hidden_in, partial[0], [got[0], got[2], got[1]])
    moved = lax.all_to_all(sent, "rep", split_axis=0, concat_axis=0, tiled=True)
    sums = feed(gather_block(one, two), w_in, w_down, fed)
    down_sum = scatter_block(sums, local_rows // 2)

    cache_out = pick(moved, source)
    first_row = (row * 4 + column) * local_rows
    within = first_row % span + jnp.arange(local_rows, dtype=jnp.int32)
    live = within < lax.dynamic_index_in_dim(spans, first_row // span, keepdims=False)
    hidden_out = jnp.where(live[:, None], middle.astype(jnp.float32) + down_sum, 0.0)
    return (
        hidden_out.astype(jnp.bfloat16),
        cache_out.reshape(slots, kinds, stored + span, 1, size),
    )


def solution(mesh):
    in_specs = (
        P(("rep", "row", "col"), None),
        P(None, ("row", "col"), None),
        P(("row", "col"), None, None),
        P(None, None, ("row", "col")),
        P(("row", "col"), None),
        P("rep", None, None, ("row", "col"), None),
        P(),
        P(),
        P(),
    )
    out_specs = (P(("rep", "row", "col"), None), P("rep", None, None, ("row", "col"), None))
    return jax.shard_map(body, mesh=mesh, in_specs=in_specs, out_specs=out_specs, check_vma=False)
```

```python
import math

import jax
import jax.numpy as jnp
import numpy as np
from jax import lax
from jax.experimental import pallas as pl
from jax.experimental.pallas import tpu as pltpu
from jax.sharding import PartitionSpec as P

EPSILON = 1e-05


def layer_norm(values):
    centred = values - jnp.mean(values, axis=-1, keepdims=True)
    spread = jnp.mean(centred * centred, axis=-1, keepdims=True)
    return centred * lax.rsqrt(spread + EPSILON)


def swap(axis, k, array):
    size = lax.axis_size(axis)
    return lax.ppermute(array, axis, [(i, i ^ k) for i in range(size)])


def together(sent):
    got = [swap(axis, k, array) for axis, k, array in sent]
    return lax.optimization_barrier(got)


def join(pieces):
    return lax.optimization_barrier(jnp.concatenate(pieces, axis=0))


def gather_plane(one, two, two_more):
    sent = [("col", 1, one), ("row", 1, two), ("col", 3, one), ("row", 3, two)]
    got = together(sent + [("col", 2, one), ("row", 2, two_more)])
    tall = two.shape[0]
    more = got[5][tall:]
    one = join([one, got[0], got[4], got[2]])
    two = join([two, got[1], got[5][:tall], got[3]])
    got = together([x for k in (2, 3, 1) for x in (("row", k, one), ("col", k, two))])
    return [one, got[4], got[0], got[2], two, got[5], got[1], got[3]], more


def gather_block(one, two):
    got = together([("col", 1, one), ("row", 1, two), ("col", 3, one), ("col", 2, one)])
    two = join([two, got[1]])
    one = join([one, got[0], got[3], got[2]])
    got = together([("col", 1, two), ("row", 1, one), ("col", 3, two), ("col", 2, two)])
    return [one, got[1], two, got[0], got[3], got[2]]


def wide_sum(arrays):
    total = arrays[0].astype(jnp.float32)
    for array in arrays[1:]:
        total = total + array.astype(jnp.float32)
    return total


def scatter_block(sums, half):
    one, two = sums[:2], sums[2:]
    got = together([("col", 1, two[1]), ("row", 1, one[1]), ("col", 3, two[3]), ("col", 2, two[2])])
    one = wide_sum([one[0], got[1]]).astype(jnp.bfloat16)
    two = wide_sum([two[0], got[0], got[3], got[2]]).astype(jnp.bfloat16)
    one = [one[half * n : half * (n + 1)] for n in range(4)]
    two = [two[half * n : half * (n + 1)] for n in range(2)]
    got = together([("col", 1, one[1]), ("row", 1, two[1]), ("col", 3, one[3]), ("col", 2, one[2])])
    return jnp.concatenate(
        [wide_sum([one[0], got[0], got[3], got[2]]), wide_sum([two[0], got[1]])], axis=0
    )


def norm_kernel(rows_ref, one_ref, two_ref):
    half = one_ref.shape[0]
    normed = layer_norm(rows_ref[...].astype(jnp.float32)).astype(jnp.bfloat16)
    one_ref[...] = normed[:half]
    two_ref[...] = normed[half:]


def norm(rows):
    part = jax.ShapeDtypeStruct((rows.shape[0] // 2, rows.shape[1]), jnp.bfloat16)
    return pl.pallas_call(
        norm_kernel,
        out_shape=(part, part),
        compiler_params=pltpu.CompilerParams(vmem_limit_bytes=4 << 20),
        cost_estimate=pl.CostEstimate(
            flops=8 * rows.size, transcendentals=0, bytes_accessed=4 * rows.size
        ),
        name="norm",
    )(rows)


def mid_kernel(rows_ref, own_ref, a_ref, b_ref, c_ref, middle_ref, one_ref, two_ref):
    half = one_ref.shape[0]
    attention = wide_sum([own_ref[...], a_ref[...], b_ref[...], c_ref[...]])
    middle = (rows_ref[...].astype(jnp.float32) + attention).astype(jnp.bfloat16)
    middle_ref[...] = middle
    normed = layer_norm(middle.astype(jnp.float32)).astype(jnp.bfloat16)
    one_ref[...] = normed[:half]
    two_ref[...] = normed[half:]


def mid(rows, own, others):
    half, width = rows.shape[0] // 2, rows.shape[1]
    part = jax.ShapeDtypeStruct((half, width), jnp.bfloat16)
    return pl.pallas_call(
        mid_kernel,
        out_shape=(jax.ShapeDtypeStruct(rows.shape, jnp.bfloat16), part, part),
        compiler_params=pltpu.CompilerParams(vmem_limit_bytes=6 << 20),
        cost_estimate=pl.CostEstimate(
            flops=12 * rows.size, transcendentals=0, bytes_accessed=14 * rows.size
        ),
        name="mid",
    )(rows, own, *others)


def joined_kernel(*refs):
    pieces, (heads_ref, out_ref, rows_ref) = refs[:8], refs[8:]
    tall = pieces[0].shape[0]
    for n in range(0, len(pieces), 4):
        for m in range(4):
            rows_ref[pl.ds(tall * m, tall), :] = pieces[n + m][...]
        out_ref[pl.ds(tall * n, 4 * tall), :] = jnp.dot(
            rows_ref[...], heads_ref[...], preferred_element_type=jnp.float32
        )


def join_heads(pieces, heads):
    tall, width = pieces[0].shape
    shape = (len(pieces) * tall, heads.shape[1])
    in_vmem = pl.BlockSpec(memory_space=pltpu.VMEM)
    return pl.pallas_call(
        joined_kernel,
        out_shape=jax.ShapeDtypeStruct(shape, jnp.float32),
        in_specs=[in_vmem] * (len(pieces) + 1),
        out_specs=in_vmem,
        scratch_shapes=[pltpu.VMEM((4 * tall, width), jnp.bfloat16)],
        compiler_params=pltpu.CompilerParams(vmem_limit_bytes=10 << 20),
        cost_estimate=pl.CostEstimate(
            flops=2 * shape[0] * width * shape[1], transcendentals=0, bytes_accessed=7 << 20
        ),
        name="join_heads",
    )(*pieces, heads)


def project_kernel(*refs):
    parts, fed_ref, outs = refs[:4], refs[4], refs[5:9]
    heads_ref, weight_ref, sems = refs[9:]
    shares = fed_ref.shape[0]
    tall = weight_ref.shape[0] // shares
    copies = [
        pltpu.make_async_copy(
            fed_ref.at[r, pl.ds(0, tall)], weight_ref.at[pl.ds(tall * r, tall)], sems.at[r]
        )
        for r in range(shares)
    ]
    for copy in copies:
        copy.start()
    size = parts[0].shape[1]
    for n, part in enumerate(parts):
        heads_ref[:, size * n : size * (n + 1)] = part[...]
    for copy in copies:
        copy.wait()
    step = 512

    @pl.loop(0, weight_ref.shape[1] // step)
    def _(j):
        span = pl.ds(pl.multiple_of(step * j, step), step)
        total = jnp.dot(
            heads_ref[...], weight_ref[:, span], preferred_element_type=jnp.float32
        ).astype(jnp.bfloat16)
        for n, out in enumerate(outs):
            out[:, span] = total[out.shape[0] * n : out.shape[0] * (n + 1)]


def project(parts, fed, local_rows):
    rows, size = parts[0].shape
    width = fed.shape[2]
    in_vmem = pl.BlockSpec(memory_space=pltpu.VMEM)
    return pl.pallas_call(
        project_kernel,
        out_shape=[jax.ShapeDtypeStruct((local_rows, width), jnp.bfloat16)] * 4,
        in_specs=[in_vmem] * 4 + [pl.BlockSpec(memory_space=pltpu.HBM)],
        out_specs=[in_vmem] * 4,
        scratch_shapes=[
            pltpu.VMEM((rows, 4 * size), jnp.bfloat16),
            pltpu.VMEM((4 * size, width), jnp.bfloat16),
            pltpu.SemaphoreType.DMA((fed.shape[0],)),
        ],
        compiler_params=pltpu.CompilerParams(vmem_limit_bytes=10 << 20),
        cost_estimate=pl.CostEstimate(
            flops=8 * rows * size * width, transcendentals=0, bytes_accessed=4 << 20
        ),
        name="project",
    )(*parts, fed)


def feed_kernel(*refs):
    pieces, (w_in_ref, w_down_ref, fed_ref), outs = refs[:6], refs[6:9], refs[9:15]
    rows_ref, in_ref, down_ref, hidden_ref, sems = refs[15:]
    units, width = w_down_ref.shape
    shares, tall, _ = fed_ref.shape
    part_in, part_down = width // shares, units // shares
    first = tall - part_in // 2 - part_down
    half = width // 2
    jobs = []
    for r in range(shares):
        for n in range(2):
            jobs.append(
                (
                    fed_ref.at[r, pl.ds(first, part_in // 2), pl.ds(half * n, half)],
                    in_ref.at[pl.ds(part_in * r + part_in // 2 * n, part_in // 2)],
                )
            )
        jobs.append(
            (
                fed_ref.at[r, pl.ds(tall - part_down, part_down)],
                down_ref.at[pl.ds(part_down * r, part_down)],
            )
        )
    copies = [
        pltpu.make_async_copy(source, target, sems.at[n])
        for n, (source, target) in enumerate(jobs)
    ]
    for copy in copies:
        copy.start()
    at = 0
    for piece in pieces:
        rows_ref[pl.ds(at, piece.shape[0]), :] = piece[...]
        at += piece.shape[0]
    step = 256
    for shard, weight_ref in enumerate((w_in_ref, in_ref)):
        if shard == 1:
            for copy in copies:
                copy.wait()

        @pl.loop(0, units // step)
        def _(j):
            at = pl.multiple_of(step * j, step)
            gate = jnp.dot(
                rows_ref[...],
                weight_ref[:, pl.ds(at, step)],
                preferred_element_type=jnp.float32,
            )
            up = jnp.dot(
                rows_ref[...],
                weight_ref[:, pl.ds(pl.multiple_of(units + at, step), step)],
                preferred_element_type=jnp.float32,
            )
            hidden = gate / (1.0 + jnp.exp(-gate)) * up
            hidden_ref[shard, :, pl.ds(at, step)] = hidden.astype(jnp.bfloat16)

    @pl.loop(0, width // step)
    def _(j):
        span = pl.ds(pl.multiple_of(step * j, step), step)
        total = jnp.dot(
            hidden_ref[0], w_down_ref[:, span], preferred_element_type=jnp.float32
        ) + jnp.dot(hidden_ref[1], down_ref[:, span], preferred_element_type=jnp.float32)
        total = total.astype(jnp.bfloat16)
        at = 0
        for out in outs:
            out[:, span] = total[at : at + out.shape[0]]
            at += out.shape[0]


def feed(pieces, w_in, w_down, fed):
    units, width = w_down.shape
    rows = sum(piece.shape[0] for piece in pieces)
    return pl.pallas_call(
        feed_kernel,
        out_shape=[jax.ShapeDtypeStruct(piece.shape, jnp.bfloat16) for piece in pieces],
        in_specs=[pl.BlockSpec(memory_space=pltpu.VMEM)] * (len(pieces) + 2)
        + [pl.BlockSpec(memory_space=pltpu.HBM)],
        out_specs=[pl.BlockSpec(memory_space=pltpu.VMEM)] * len(pieces),
        scratch_shapes=[
            pltpu.VMEM((rows, width), jnp.bfloat16),
            pltpu.VMEM((width, 2 * units), jnp.bfloat16),
            pltpu.VMEM((units, width), jnp.bfloat16),
            pltpu.VMEM((2, rows, units), jnp.bfloat16),
            pltpu.SemaphoreType.DMA((3 * fed.shape[0],)),
        ],
        compiler_params=pltpu.CompilerParams(vmem_limit_bytes=18 << 20),
        cost_estimate=pl.CostEstimate(
            flops=12 * rows * width * units, transcendentals=2 * rows * units,
            bytes_accessed=16 << 20,
        ),
        name="feed",
    )(*pieces, w_in, w_down, fed)


def attend_one(
    request, away, column, length_old, span_new,
    joined_ref, cache_ref, cos_ref, sin_ref, far_cos_ref, far_sin_ref, new_ref,
):
    columns = [column ^ (2 * (request % 2) + n) for n in range(2)]

    def block(n):
        return joined_ref[pl.ds(pl.multiple_of(32 * n, 32), 32), :]

    joined = jnp.concatenate(
        [block(n) for c in columns for n in (4 * away + c, 16 + 4 * c + away)], axis=0
    )
    far_cos, far_sin = far_cos_ref[pl.ds(request, 1), :], far_sin_ref[pl.ds(request, 1), :]
    cosine = far_cos * cos_ref[...] - far_sin * sin_ref[...]
    sine = far_sin * cos_ref[...] + far_cos * sin_ref[...]

    def turned(part):
        return (part * cosine + pltpu.roll(part, 64, axis=1) * sine).astype(jnp.bfloat16)

    queries = turned(joined[:, :128])
    keys_new = turned(joined[:, 128:256])
    values_new = joined[:, 256:].astype(jnp.bfloat16)
    stored, whole = cache_ref.shape[1], new_ref.shape[1]
    live = lax.broadcasted_iota(jnp.int32, keys_new.shape, 0) < span_new
    rows = lax.broadcasted_iota(jnp.int32, (whole, keys_new.shape[1]), 0)
    for kind, fresh in enumerate((keys_new, values_new)):
        fresh = jnp.where(live, fresh.astype(jnp.float32), 0.0)
        fresh = jnp.concatenate(
            [fresh, jnp.zeros((whole - fresh.shape[0], fresh.shape[1]), jnp.float32)], axis=0
        )
        old = cache_ref[kind].astype(jnp.float32)
        old = jnp.concatenate(
            [old, jnp.zeros((whole - stored, old.shape[1]), jnp.float32)], axis=0
        )
        fresh = pltpu.roll(fresh, length_old, axis=0)
        new_ref[kind] = jnp.where(rows < length_old, old, fresh).astype(jnp.bfloat16)
    scale = 1.0 / math.sqrt(128)
    contract = (((1,), (1,)), ((), ()))
    old = (
        lax.dot_general(queries, cache_ref[0], contract, preferred_element_type=jnp.float32)
        * scale
    )
    new = (
        lax.dot_general(queries, keys_new, contract, preferred_element_type=jnp.float32) * scale
    )
    old_ok = lax.broadcasted_iota(jnp.int32, old.shape, 1) < length_old
    new_ok = lax.broadcasted_iota(jnp.int32, new.shape, 1) <= lax.broadcasted_iota(
        jnp.int32, new.shape, 0
    )
    old = jnp.where(old_ok, old, -1e30)
    new = jnp.where(new_ok, new, -1e30)
    highest = jnp.maximum(
        jnp.max(old, axis=1, keepdims=True), jnp.max(new, axis=1, keepdims=True)
    )
    old = jnp.where(old_ok, jnp.exp(old - highest), 0.0)
    new = jnp.where(new_ok, jnp.exp(new - highest), 0.0)
    total = jnp.sum(old, axis=1, keepdims=True) + jnp.sum(new, axis=1, keepdims=True)
    context = jnp.dot(
        (old / total).astype(jnp.bfloat16), cache_ref[1], preferred_element_type=jnp.float32
    ) + jnp.dot(
        (new / total).astype(jnp.bfloat16), values_new, preferred_element_type=jnp.float32
    )
    return context.astype(jnp.bfloat16), columns


def attend_kernel(
    place_ref, length_ref, span_ref, target_ref,
    joined_ref, cache_ref, cos_ref, sin_ref, far_cos_ref, far_sin_ref, *refs,
):
    contexts, (sent_ref, held_ref, sems) = refs[:4], refs[4:]
    step = pl.program_id(0)
    column = place_ref[1]
    source_row = place_ref[0] ^ step

    def copy_of(n, target):
        return pltpu.make_async_copy(held_ref.at[n], sent_ref.at[target], sems.at[n])

    for m in range(2):
        request = 2 * source_row + m
        context, columns = attend_one(
            request, step, column, length_ref[request], span_ref[request],
            joined_ref, cache_ref.at[m], cos_ref, sin_ref, far_cos_ref, far_sin_ref,
            held_ref.at[2 * step + m],
        )
        for n in range(2):
            for q in range(4):

                @pl.when(step == q)
                def _():
                    at = pl.multiple_of(64 * columns[n], 64)
                    contexts[q][pl.ds(at, 64), :] = context[64 * n : 64 * n + 64]

        copy_of(2 * step + m, target_ref[request]).start()

    @pl.when(step == 3)
    def _():
        for n in range(8):
            copy_of(n, target_ref[2 * (place_ref[0] ^ (n // 2)) + n % 2]).wait()


def attend(place, lengths, spans, targets, joined, cache, tables, replicas):
    slots, kinds, stored, size = cache.shape
    span = tables[0].shape[0]
    in_vmem = pl.BlockSpec(memory_space=pltpu.VMEM)
    context = jax.ShapeDtypeStruct((slots // 4 * span, size), jnp.bfloat16)
    return pl.pallas_call(
        attend_kernel,
        out_shape=[context] * 4
        + [pltpu.HBM((replicas, kinds, stored + span, size), jnp.bfloat16)],
        grid_spec=pltpu.PrefetchScalarGridSpec(
            num_scalar_prefetch=4,
            grid=(4,),
            in_specs=[
                in_vmem,
                pl.BlockSpec(
                    (slots // 4, kinds, stored, size),
                    lambda step, place, *refs: (place[0] ^ step, 0, 0, 0),
                ),
            ]
            + [in_vmem] * len(tables),
            out_specs=[in_vmem] * 4 + [pl.BlockSpec(memory_space=pltpu.HBM)],
            scratch_shapes=[
                pltpu.VMEM((slots, kinds, stored + span, size), jnp.bfloat16),
                pltpu.SemaphoreType.DMA((slots,)),
            ],
        ),
        compiler_params=pltpu.CompilerParams(vmem_limit_bytes=12 << 20),
        cost_estimate=pl.CostEstimate(
            flops=4 * slots * span * (stored + span) * size,
            transcendentals=slots * span * (stored + span),
            bytes_accessed=6 << 20,
        ),
        name="attend",
    )(place, lengths, spans, targets, joined, cache, *tables)


def pick_kernel(source_ref, moved_ref, out_ref, held_ref, sems):
    slots = out_ref.shape[0]
    taken = [
        pltpu.make_async_copy(moved_ref.at[source_ref[t]], held_ref.at[t], sems.at[0, t])
        for t in range(slots)
    ]
    given = [
        pltpu.make_async_copy(held_ref.at[t], out_ref.at[t], sems.at[1, t]) for t in range(slots)
    ]
    for copy in taken:
        copy.start()
    for t in range(slots):
        taken[t].wait()
        given[t].start()
    for copy in given:
        copy.wait()


def pick(moved, source):
    shape = (source.shape[0],) + moved.shape[1:]
    return pl.pallas_call(
        pick_kernel,
        out_shape=jax.ShapeDtypeStruct(shape, moved.dtype),
        in_specs=[pl.BlockSpec(memory_space=pltpu.SMEM), pl.BlockSpec(memory_space=pltpu.HBM)],
        out_specs=pl.BlockSpec(memory_space=pltpu.HBM),
        scratch_shapes=[pltpu.VMEM(shape, moved.dtype), pltpu.SemaphoreType.DMA((2, shape[0]))],
        cost_estimate=pl.CostEstimate(
            flops=0, transcendentals=0, bytes_accessed=4 * math.prod(shape)
        ),
        name="pick",
    )(source, moved)


def body(hidden_in, w_qkv, w_out, w_gate_up, w_down, cache, span_len, cache_len, new_slot):
    slots, kinds, stored, _, size = cache.shape
    local_rows, width = hidden_in.shape
    units = w_down.shape[0]
    span = 16 * local_rows // slots
    replica = lax.axis_index("rep")
    replicas = lax.axis_size("rep")
    row, column = lax.axis_index("row"), lax.axis_index("col")
    cache = cache.reshape(slots, kinds, stored, size)
    lengths = lax.dynamic_slice_in_dim(cache_len, replica * slots, slots)
    spans = lax.dynamic_slice_in_dim(span_len, replica * slots, slots)
    targets = lax.dynamic_slice_in_dim(new_slot, replica * slots, slots) // slots
    my_slots = replica * slots + jnp.arange(slots, dtype=jnp.int32)
    arrivals = (new_slot[None, :] == my_slots[:, None]).astype(jnp.int32)
    requests = jnp.arange(new_slot.shape[0], dtype=jnp.int32)
    source = jnp.sum(arrivals * (requests // slots)[None, :], axis=1)

    one, two = norm(hidden_in)
    one, two, w_gate_up = lax.optimization_barrier((one, two, w_gate_up))

    out_rows = 4 * size // replicas
    out_slice = lax.dynamic_slice_in_dim(
        w_out.reshape(size, width), out_rows * (replica % (size // out_rows)), out_rows
    )
    per_head = size // out_rows
    pairs = [
        (4 * r + i, 4 * r + (i ^ (r // per_head))) for r in range(replicas) for i in range(4)
    ]
    out_far = lax.ppermute(out_slice, ("rep", "row"), pairs)
    rows_in, rows_down = width // replicas, units // replicas
    in_slice = lax.dynamic_slice_in_dim(w_gate_up, replica * rows_in, rows_in)
    in_slice = in_slice.reshape(2, rows_in // 2, 2 * units)
    down_slice = lax.dynamic_slice_in_dim(w_down, replica * rows_down, rows_down)
    two_more = jnp.concatenate(
        [two, jnp.concatenate([in_slice[0], in_slice[1]], axis=1), down_slice], axis=0
    )

    one, two, two_more, out_far = lax.optimization_barrier((one, two, two_more, out_far))
    pieces, feed_far = gather_plane(one, two, two_more)
    fed = lax.all_gather(
        jnp.concatenate([out_far, feed_far], axis=0), "rep", axis=0, tiled=False
    )
    w_in = w_gate_up.reshape(width, 2 * units)
    pieces, w_in = lax.optimization_barrier((pieces, w_in))
    joined = join_heads(pieces, w_qkv.reshape(width, 3 * size))

    frequency = 10000.0 ** (-(np.arange(size // 2) * 2.0 / size))
    frequency = np.concatenate([frequency, frequency])[None, :]
    sign = np.where(np.arange(size) < size // 2, -1.0, 1.0)[None, :]
    near = np.arange(span)[:, None] * frequency
    far = lengths.astype(jnp.float32)[:, None] * jnp.asarray(frequency, jnp.float32)
    tables = (
        jnp.asarray(np.cos(near), jnp.float32),
        jnp.asarray(np.sin(near) * sign, jnp.float32),
        jnp.cos(far),
        jnp.sin(far) * jnp.asarray(sign, jnp.float32),
    )
    place = jnp.stack([row, column]).astype(jnp.int32)
    *context, sent = attend(place, lengths, spans, targets, joined, cache, tables, replicas)

    got, sent = lax.optimization_barrier(([swap("row", k, context[k]) for k in (1, 3, 2)], sent))
    fed = pltpu.with_memory_space_constraint(fed, pltpu.HBM)
    partial = project([context[0], got[0], got[2], got[1]], fed, local_rows)
    got = together([("col", k, partial[k]) for k in (1, 3, 2)])
    middle, one, two = mid(hidden_in, partial[0], [got[0], got[2], got[1]])
    moved = lax.all_to_all(sent, "rep", split_axis=0, concat_axis=0, tiled=True)
    sums = feed(gather_block(one, two), w_in, w_down, fed)
    down_sum = scatter_block(sums, local_rows // 2)

    cache_out = pick(moved, source)
    first_row = (row * 4 + column) * local_rows
    within = first_row % span + jnp.arange(local_rows, dtype=jnp.int32)
    live = within < lax.dynamic_index_in_dim(spans, first_row // span, keepdims=False)
    hidden_out = jnp.where(live[:, None], middle.astype(jnp.float32) + down_sum, 0.0)
    return (
        hidden_out.astype(jnp.bfloat16),
        cache_out.reshape(slots, kinds, stored + span, 1, size),
    )


def solution(mesh):
    in_specs = (
        P(("rep", "row", "col"), None),
        P(None, ("row", "col"), None),
        P(("row", "col"), None, None),
        P(None, None, ("row", "col")),
        P(("row", "col"), None),
        P("rep", None, None, ("row", "col"), None),
        P(),
        P(),
        P(),
    )
    out_specs = (P(("rep", "row", "col"), None), P("rep", None, None, ("row", "col"), None))
    return jax.shard_map(body, mesh=mesh, in_specs=in_specs, out_specs=out_specs, check_vma=False)
```
